32 devices in a mesh: tm: 4 (over z), row: 8 (over y, x, core).
Axes of the slice: x: 2, y: 2, z: 4, core: 2. Of those that a mesh axis runs over, the one named last changes fastest.
Arguments:
- features: bfloat16 [16, 32, 64, 512], P('tm', 'row'), may hold values from -200 to 200
- norm_gain: float32 [512], replicated, may hold values from 0.1 to 1.9
- norm_bias: float32 [512], replicated, may hold values from -3 to 3
- latent_kernel: bfloat16 [16, 3, 3, 3, 512], replicated, may hold values from -0.0546875 to 0.0546875
- latent_bias: float32 [16], replicated, may hold values from -3 to 3
- token_mask: int32 [16, 32, 64], P('tm', 'row'), may hold values 0 or 1
- embed_weight: bfloat16 [16, 2048], replicated, may hold values from -1.5 to 1.5
- mask_token: float32 [2048], replicated, may hold values from -5 to 5
- pos_embed: bfloat16 [16, 32, 64, 2048], P('tm', 'row'), may hold values from -3 to 3
- query_weight: bfloat16 [2048, 1024], replicated, may hold values from -0.125 to 0.125
- key_weight: bfloat16 [2048, 1024], replicated, may hold values from -0.125 to 0.125
- value_weight: bfloat16 [2048, 1024], replicated, may hold values from -0.125 to 0.125
- logit_scale: float32 [8], replicated, may hold values from 8 to 32
- pattern: int32 [16, 16, 4], P('tm', 'row'), may hold values from -1 to 255, as said below
Outputs:
- attended: bfloat16 [16, 32, 64, 1024], P('tm', 'row')
The draws below stay inside these ranges and needn't reach their ends.
Inputs may be any that keep to these rules, and one draw needn't show every extreme that they name: `pattern`: row (t, p) lists key blocks for the query block of frame t and row pair p (block id t * 16 + p): first that block itself, then distinct blocks whose frame differs from t by at most one and whose row pair differs from p by at most one; the rest of the row is -1. On every device the first row pair of its first frame lists 4 blocks.
All inputs are finite; a program needn't handle non-finite values. No bound on the sum of `token_mask` on one device may be relied on, other than what follows from the above.
Results may differ from the reference program's by a relative error of at most 0.0085.
Values may be sent and summed in bfloat16 or wider, within the bound.
No kernel may reach another device: no remote copies, remote signals or barrier semaphores. Data moves between devices by JAX's collectives and lax.ppermute only.
A program may use at most 128 MiB of HBM per device.

```python
import math
import jax
import jax.numpy as jnp
from jax import lax

C = 512
LAT = 16
D = 2048
HEADS = 8
HD = 128
GROUPS = 32
MAXKB = 4
FT = 4
FR = 4
NW = 64
NT = 16
NH = 32


def draw_features(key, part):
    streams = jax.random.split(key, 4)
    frame_pos = jnp.arange(NT).astype(jnp.float32) / max(NT - 1, 1)
    rising = (3.0 ** frame_pos)[:, None, None, None]
    row_scale = jnp.exp(jax.random.uniform(streams[0], (NT, NH, 1, 1)) * math.log(3.0))
    noise = jax.random.normal(streams[1], (NT, NH, NW, C))
    channel_scale = jnp.exp(jax.random.uniform(streams[2], (C,)) * math.log(3.0))
    channel_mean = 0.5 * jax.random.normal(streams[3], (C,))
    return jnp.clip(channel_mean + rising * row_scale * channel_scale * noise, -200.0, 200.0).astype(jnp.bfloat16)


def draw_pattern(key, part):
    pair_total = NH // 2
    first_key, second_key = jax.random.split(key)
    frame_ids = jnp.arange(NT)[:, None, None]
    pair_ids = jnp.arange(pair_total)[None, :, None]
    frame_steps = jnp.array([-1, -1, -1, 0, 0, 1, 1, 1], jnp.int32)
    pair_steps = jnp.array([-1, 0, 1, -1, 1, -1, 0, 1], jnp.int32)
    key_frame = frame_ids + frame_steps
    key_pair = pair_ids + pair_steps
    inside = (key_frame >= 0) & (key_frame < NT) & (key_pair >= 0) & (key_pair < pair_total)
    random_rank = jax.random.randint(first_key, (NT, pair_total, 8), 0, 1 << 20) * 8 + jnp.arange(8)
    ranking = jnp.where(inside, random_rank, (1 << 24) + jnp.arange(8))
    ordering = jnp.argsort(ranking, axis=-1)
    neighbour_ids = jnp.take_along_axis(key_frame * pair_total + key_pair, ordering, axis=-1)
    inside_count = jnp.sum(inside.astype(jnp.int32), axis=-1)
    listed_count = jax.random.randint(second_key, (NT, pair_total), 1, MAXKB + 1)
    leading = (frame_ids[..., 0] % FT == 0) & (pair_ids[..., 0] % (FR // 2) == 0)
    listed_count = jnp.where(leading, MAXKB, listed_count)
    listed_count = jnp.minimum(listed_count, 1 + inside_count)
    own_ids = frame_ids[..., 0] * pair_total + pair_ids[..., 0]
    entries = jnp.concatenate([own_ids[..., None], neighbour_ids[..., :MAXKB - 1]], axis=-1)
    live_slot = jnp.arange(MAXKB)[None, None, :] < listed_count[..., None]
    return jnp.where(live_slot, entries, -1).astype(jnp.int32)


def place_ends(result, rng, smallest, high):
    longest = result.shape.index(max(result.shape))
    spots = []
    for shift in (0, 1):
        where = [jax.random.randint(jax.random.fold_in(rng, axis), (), 0, length) for axis, length in enumerate(result.shape)]
        where[longest] = (where[longest] + shift) % result.shape[longest]
        spots.append(tuple(where))
    return result.at[spots[0]].set(smallest).at[spots[1]].set(high)


def level_of(key, shape, pieces, smallest, top_value):
    def one(dim, shards_of):
        draws = jax.random.uniform(jax.random.fold_in(jax.random.fold_in(key, 6), dim), (shards_of,), jnp.float32, smallest / len(pieces), top_value / len(pieces))
        return jnp.repeat(jnp.exp(draws), shape[dim] // shards_of).reshape((-1,) + (1,) * (len(shape) - dim - 1))

    gain = one(*pieces[0])
    for cut in pieces[1:]:
        gain = gain * one(*cut)
    return gain


def scatter_about(own_key, shape, deviation, reach, cuts=(), kind=jnp.bfloat16):
    values = jax.random.normal(own_key, shape, jnp.float32) * deviation
    if len(cuts) > 0:
        values = level_of(own_key, shape, cuts, -0.22, 0.18) * values
    return jnp.clip(values, min=-reach, max=reach).astype(kind)


def setup_inputs(seed: int = 0) -> dict:
    streams_of = jax.random.split(jax.random.key(seed), 15)
    features = draw_features(jax.random.fold_in(streams_of[14], 71), 0)
    norm_gain = jnp.clip(1.0 + 0.18 * jax.random.normal(streams_of[1], (C,), jnp.float32), 0.1, 1.9)
    norm_bias = scatter_about(streams_of[2], (C,), 0.5, 3.0, (), jnp.float32)
    latent_kernel = scatter_about(streams_of[3], (LAT, 3, 3, 3, C), (27 * C) ** -0.5, 0.0546875)
    latent_bias = scatter_about(streams_of[4], (LAT,), 0.5, 3.0, (), jnp.float32)
    token_mask = place_ends((jax.random.randint(streams_of[5], (NT, NH, NW), 0, 4) < 1).astype(jnp.int32), jax.random.fold_in(streams_of[5], 1), 0, 1)
    embed_weight = scatter_about(streams_of[6], (LAT, D), LAT ** -0.5, 1.5)
    mask_token = scatter_about(streams_of[7], (D,), 1.0, 5.0, (), jnp.float32)
    pos_embed = scatter_about(streams_of[8], (NT, NH, NW, D), 0.5, 3.0, ((0, 4), (1, 8)))
    query_weight = scatter_about(streams_of[9], (D, HEADS * HD), D ** -0.5, 0.125)
    key_weight = scatter_about(streams_of[10], (D, HEADS * HD), D ** -0.5, 0.125)
    value_weight = scatter_about(streams_of[11], (D, HEADS * HD), D ** -0.5, 0.125)
    logit_scale = jnp.clip(jnp.exp(jax.random.uniform(streams_of[12], (HEADS,), jnp.float32, math.log(8.0), math.log(32.0))), 8.0, 32.0)
    pattern = draw_pattern(jax.random.fold_in(streams_of[14], 71), 0)
    return {"features": features, "norm_gain": norm_gain, "norm_bias": norm_bias, "latent_kernel": latent_kernel, "latent_bias": latent_bias, "token_mask": token_mask, "embed_weight": embed_weight, "mask_token": mask_token, "pos_embed": pos_embed, "query_weight": query_weight, "key_weight": key_weight, "value_weight": value_weight, "logit_scale": logit_scale, "pattern": pattern}


def unit_heads(values, head_count):
    shaped = values.astype(jnp.float32).reshape(values.shape[0], head_count, -1)
    normal = shaped * lax.rsqrt(lax.optimization_barrier(jnp.mean(shaped * shaped, axis=-1, keepdims=True)) + 1e-06)
    return normal.astype(jnp.bfloat16).reshape(values.shape[0], -1)

def reference(features, norm_gain, norm_bias, latent_kernel, latent_bias, token_mask, embed_weight, mask_token, pos_embed, query_weight, key_weight, value_weight, logit_scale, pattern):
    frames, slab_rows, row_width, channels = features.shape
    per_group = channels // GROUPS
    widened = features.astype(jnp.float32)
    grouped = widened.reshape(-1, GROUPS, per_group)
    totals = lax.optimization_barrier(jnp.sum(grouped, axis=(0, 2)))
    squares = lax.optimization_barrier(jnp.sum(grouped * grouped, axis=(0, 2)))
    cell_count = frames * slab_rows * row_width * per_group
    average = totals / cell_count
    variance = squares / cell_count - average * average
    inverse = lax.rsqrt(variance + 1e-06)
    channel_scale = jnp.repeat(inverse, per_group) * norm_gain
    channel_shift = norm_bias - jnp.repeat(average * inverse, per_group) * norm_gain
    activated = jax.nn.silu(widened * channel_scale + channel_shift).astype(jnp.bfloat16)
    padded = jnp.pad(activated, ((1, 1), (1, 1), (1, 1), (0, 0)))
    summed = jnp.zeros((frames * slab_rows * row_width, LAT), jnp.float32)
    for offset_t in range(3):
        for offset_h in range(3):
            for offset_w in range(3):
                window = padded[offset_t:offset_t + frames, offset_h:offset_h + slab_rows, offset_w:offset_w + row_width]
                summed = summed + jnp.dot(window.reshape(-1, channels), latent_kernel[:, offset_t, offset_h, offset_w, :].T, preferred_element_type=jnp.float32)
    latent = (summed + latent_bias).astype(jnp.bfloat16)
    tokens = jnp.dot(latent, embed_weight, preferred_element_type=jnp.float32)
    tokens = jnp.where(token_mask.reshape(-1, 1) == 1, mask_token, tokens)
    tokens = tokens + pos_embed.reshape(-1, pos_embed.shape[-1]).astype(jnp.float32)
    centred = tokens - lax.optimization_barrier(jnp.mean(tokens, axis=-1, keepdims=True))
    hidden = (centred * lax.rsqrt(lax.optimization_barrier(jnp.mean(centred * centred, axis=-1, keepdims=True)) + 1e-05)).astype(jnp.bfloat16)
    unit_query = unit_heads(jnp.dot(hidden, query_weight, preferred_element_type=jnp.float32).astype(jnp.bfloat16), HEADS)
    unit_key = unit_heads(jnp.dot(hidden, key_weight, preferred_element_type=jnp.float32).astype(jnp.bfloat16), HEADS)
    value_raw = jnp.dot(hidden, value_weight, preferred_element_type=jnp.float32).astype(jnp.bfloat16)
    pair_total = slab_rows // 2
    block_span = 2 * row_width
    inner = HEADS * HD
    query_blocks = unit_query.reshape(frames, pair_total, block_span, HEADS, HD)
    key_blocks = unit_key.reshape(frames * pair_total, block_span, inner)
    value_blocks = value_raw.reshape(frames * pair_total, block_span, inner)
    scale = logit_scale / HD

    def one_frame(inputs):
        frame_queries, frame_list = inputs
        usable = frame_list >= 0
        clamped = jnp.maximum(frame_list, 0)
        key_rows = jnp.take(key_blocks, clamped, axis=0).reshape(pair_total, MAXKB * block_span, HEADS, HD).astype(jnp.float32)
        value_rows = jnp.take(value_blocks, clamped, axis=0).reshape(pair_total, MAXKB * block_span, HEADS, HD).astype(jnp.float32)
        scores = jnp.einsum('bqhd,bkhd->bhqk', frame_queries.astype(jnp.float32), key_rows) * scale[None, :, None, None]
        live_keys = jnp.repeat(usable, block_span, axis=1).astype(jnp.float32)
        weights = jnp.exp(scores) * live_keys[:, None, None, :]
        denominator = lax.optimization_barrier(jnp.sum(weights, axis=-1))
        rounded = lax.optimization_barrier(weights.astype(jnp.bfloat16)).astype(jnp.float32)
        numerator = jnp.einsum('bhqk,bkhd->bqhd', rounded, value_rows)
        return (numerator / jnp.transpose(denominator, (0, 2, 1))[..., None]).astype(jnp.bfloat16)
    attended = lax.map(one_frame, (query_blocks, pattern))
    return attended.reshape(frames, slab_rows, row_width, inner)
```

```python
import functools

import jax
import jax.numpy as jnp
from jax import lax
from jax.experimental import pallas as pl
from jax.experimental.pallas import tpu as pltpu
from jax.sharding import PartitionSpec as P

GROUPS = 32
BF = jnp.bfloat16
F32 = jnp.float32
VM = pl.BlockSpec(memory_space=pltpu.VMEM)
SM = pl.BlockSpec(memory_space=pltpu.SMEM)
ANY = pl.BlockSpec(memory_space=pl.ANY)
AUG = 32
ONES = 19
EXT = 40
LIMIT = 58 * 1024 * 1024


def params(limit=LIMIT):
    return pltpu.CompilerParams(vmem_limit_bytes=limit)


def nt(a, b):
    return lax.dot_general(a, b, (((1,), (1,)), ((), ())), preferred_element_type=F32)


def nn(a, b):
    return lax.dot_general(a, b, (((1,), (0,)), ((), ())), preferred_element_type=F32)


def stats_kernel(x_ref, o_ref):
    @pl.when(pl.program_id(0) == 0)
    def _():
        o_ref[...] = jnp.zeros_like(o_ref)

    x = x_ref[...].astype(F32)
    o_ref[0:1] += jnp.sum(x, axis=0, keepdims=True)
    o_ref[1:2] += jnp.sum(x * x, axis=0, keepdims=True)


def side_kernel(pos_ref, embed_ref, mtok_ref, mask_ref, side_ref, mp_ref, aug_ref, am_ref, c_ref, aug):
    lat, width = embed_ref.shape
    aug[...] = jnp.zeros_like(aug)
    aug[0:lat] = embed_ref[...].astype(F32)
    m = mtok_ref[...]
    hi = m.astype(BF).astype(F32)
    mid = (m - hi).astype(BF).astype(F32)
    low = (m - hi - mid).astype(BF).astype(F32)
    aug[lat : lat + 1] = hi
    aug[lat + 1 : lat + 2] = mid
    aug[lat + 2 : lat + 3] = low
    aug[ONES : ONES + 1] = jnp.ones_like(hi)
    rows = aug[...].astype(BF)
    aug_ref[...] = rows[0:AUG]
    pos = pos_ref[...]
    d = nt(pos, rows) * (1.0 / width)
    gram = nt(rows, rows) * (1.0 / width)
    mp_ref[...] = jnp.broadcast_to(d[:, ONES : ONES + 1], d.shape)
    am_ref[...] = jnp.broadcast_to(gram[0:AUG, ONES : ONES + 1], am_ref.shape)
    sq = jnp.zeros(d.shape, F32)
    for k in range(width // 128):
        p = pos[:, k * 128 : (k + 1) * 128].astype(F32)
        sq = sq + p * p
    dt = d.T
    mean_pos = dt[ONES : ONES + 1]
    vp = jnp.sum(sq.T, axis=0, keepdims=True) * (1.0 / width) - mean_pos * mean_pos
    mean_e = gram[0:lat, ONES : ONES + 1]
    g = dt[0:lat] - mean_e * mean_pos
    mean_m = jnp.sum(gram[lat : lat + 3, ONES : ONES + 1], axis=0, keepdims=True)
    gm = jnp.sum(dt[lat : lat + 3], axis=0, keepdims=True) - mean_m * mean_pos
    c_ref[...] = gram[0:lat] - mean_e * gram[ONES : ONES + 1]
    mrow = jnp.sum(gram[lat : lat + 3], axis=0, keepdims=True)
    cm = jnp.sum(mrow[:, lat : lat + 3], axis=1, keepdims=True) - mean_m * mean_m
    masked = mask_ref[...] == 1
    side_ref[0:lat] = jnp.where(masked, 0.0, g)
    side_ref[lat : lat + 8] = jnp.concatenate(
        [
            masked.astype(F32),
            jnp.where(masked, vp + 2.0 * gm + cm, vp),
            jnp.zeros((6, mean_pos.shape[1]), F32),
        ],
        axis=0,
    )


def proj_kernel(pos_ref, aug_ref, mp_ref, am_ref, w_ref, a_ref, b_ref, r_ref, x, sem):
    tokens = pos_ref.shape[0]

    @pl.when(pl.program_id(0) == 0)
    def _():
        copy = pltpu.make_async_copy(pos_ref, x.at[pl.ds(0, tokens)], sem)
        copy.start()
        x[pl.ds(tokens, AUG), :] = aug_ref[...]
        copy.wait()

    acc = nn(x[...], w_ref[...])
    lat = 16
    aw = acc[tokens : tokens + AUG]
    colsum = aw[ONES : ONES + 1]
    ew = aw[0:lat] - am_ref[0:lat, 0:1] * colsum
    mw = jnp.sum(aw[lat : lat + 3], axis=0, keepdims=True)
    mean_m = jnp.sum(am_ref[lat : lat + 3, 0:1], axis=0, keepdims=True)
    mw = mw - mean_m * colsum
    ewh = ew.astype(BF).astype(F32)
    mwh = mw.astype(BF).astype(F32)
    r_ref[...] = jnp.concatenate(
        [ewh, ew - ewh, mwh, mw - mwh, jnp.zeros((64 - 2 * lat - 2, mw.shape[1]), F32)], axis=0
    ).astype(BF)
    frames = a_ref.shape[0]
    span = a_ref.shape[1]
    for k in range(acc.shape[1] // 128):
        cut = slice(k * 128, (k + 1) * 128)
        part = acc[0:tokens, cut] - mp_ref[...] * colsum[:, cut]
        for f in range(frames):
            a_ref[f, :, cut] = part[2 * f * span : (2 * f + 1) * span].astype(BF)
            b_ref[f, :, cut] = part[(2 * f + 1) * span : (2 * f + 2) * span].astype(BF)


def project(pos, aug, mp, am, weight, frames, span):
    tokens, width = pos.shape
    inner = weight.shape[1]
    tile = 256
    out = jax.ShapeDtypeStruct((frames, span, inner), BF)
    block = pl.BlockSpec((frames, span, tile), lambda n: (0, 0, n))
    return pl.pallas_call(
        proj_kernel,
        out_shape=(out, out, jax.ShapeDtypeStruct((64, inner), BF)),
        grid=(inner // tile,),
        in_specs=[
            ANY,
            VM,
            VM,
            VM,
            pl.BlockSpec((width, tile), lambda n: (0, n)),
        ],
        out_specs=(block, block, pl.BlockSpec((64, tile), lambda n: (0, n))),
        scratch_shapes=[pltpu.VMEM((tokens + AUG, width), BF), pltpu.SemaphoreType.DMA],
        compiler_params=params(),
        cost_estimate=pl.CostEstimate(
            flops=2 * tokens * width * inner, bytes_accessed=12 << 20, transcendentals=0
        ),
    )(pos, aug, mp, am, weight)


def conv_kernel(sum_ref, gain_ref, bias_ref, x_ref, k_ref, side_ref, o_ref, *, count, per_group, width):
    sums = sum_ref[...]
    channels = sums.shape[1]
    lane = lax.broadcasted_iota(jnp.int32, sums.shape, 1)
    step = 1
    while step < per_group:
        sums = sums + jnp.where(
            (lane & step) == 0, pltpu.roll(sums, channels - step, 1), pltpu.roll(sums, step, 1)
        )
        step *= 2
    average = sums[0:1] * (1.0 / count)
    variance = sums[1:2] * (1.0 / count) - average * average
    inverse = lax.rsqrt(variance + 1e-06)
    scale = inverse * gain_ref[...]
    shift = bias_ref[...] - average * scale
    frames = o_ref.shape[0] - 2
    lat = 16
    cells = x_ref.shape[0] // frames
    o_ref[...] = jnp.zeros_like(o_ref)
    pad = (o_ref.shape[2] - cells) // 2
    w = lax.broadcasted_iota(jnp.int32, (9 * lat, cells), 1) % width
    acc = [None] * (frames + 2)
    for f in range(frames):
        v = x_ref[f * cells : (f + 1) * cells].astype(F32) * scale + shift
        act = (v / (1.0 + jnp.exp(-v))).astype(BF)
        y = nt(k_ref[...], act)
        n = 9 * lat
        y = (
            y[n : 2 * n]
            + jnp.where(w == 0, 0.0, pltpu.roll(y[0:n], 1, 1))
            + jnp.where(w == width - 1, 0.0, pltpu.roll(y[2 * n : 3 * n], cells - 1, 1))
        )
        gap = jnp.zeros((3 * lat, pad), F32)
        m = 3 * lat
        z = [jnp.concatenate([gap, y[b * m : (b + 1) * m], gap], axis=1) for b in range(3)]
        full = z[0].shape[1]
        z = z[1] + pltpu.roll(z[0], width, 1) + pltpu.roll(z[2], full - width, 1)
        for a in range(3):
            part = z[a * lat : (a + 1) * lat]
            i = f - a + 2
            acc[i] = part if acc[i] is None else acc[i] + part
        o_ref[f + 1, lat:EXT, pad : pad + cells] = side_ref[:, f * cells : (f + 1) * cells]
    for i in range(frames + 2):
        o_ref[i, 0:lat] = acc[i]


def attend_kernel(
    slot_ref, true_ref, scale_ref,
    s_ref, zf_ref, zb_ref, bias_ref, c_ref, rk_ref, rv_ref, rq_ref, qa_ref, qb_ref,
    ka, kb, va, vb, ku, kd, vu, vd, kf, kz, vf, vz, kc, vc,
    o_ref, pk, pv, at, num, den, need, sem, *, slots,
):
    block = pl.program_id(0)
    frames = ka.shape[0]
    span = pk.shape[1]
    inner = pk.shape[2]
    heads = inner // 128
    total = pk.shape[0]
    lat = 16

    def source(j):
        f, q = j // 4 - 1, j % 4
        if 0 <= f < frames:
            k, v = ((ku, vu), (ka, va), (kb, vb), (kd, vd))[q]
            return k.at[f], v.at[f]
        late = f >= 0
        if q == 3:
            return kc.at[int(late)], vc.at[int(late)]
        where = (2, 0, 1)[q]
        return (kz.at[where], vz.at[where]) if late else (kf.at[where], vf.at[where])

    @pl.when(block == 0)
    def _():
        for j in range(total):
            need[j] = 0

        def mark(i, _):
            j = slot_ref[i]

            @pl.when(j >= 0)
            def _():
                need[j] = 1

            return 0

        lax.fori_loop(0, slot_ref.shape[0], mark, 0)
        for j in range(total):

            @pl.when(need[j] == 1)
            def _(j=j):
                k, v = source(j)
                pltpu.make_async_copy(k, pk.at[j], sem.at[0, j]).start()
                pltpu.make_async_copy(v, pv.at[j], sem.at[1, j]).start()

        c = c_ref[:, 0:lat]
        ch = c.astype(BF)
        cl = (c - ch.astype(F32)).astype(BF)
        for i in range(frames + 2):
            e = s_ref[i]
            if i < 2:
                e = e + zf_ref[i]
            if i >= frames:
                e = e + zb_ref[i - frames]
            mask = e[2 * lat : 2 * lat + 1]
            latent = (e[0:lat] + bias_ref[...]).astype(BF).astype(F32)
            latent = jnp.where(mask > 0.5, 0.0, latent)
            lb = latent.astype(BF)
            quad = nn(ch, lb) + nn(cl, lb)
            var = e[2 * lat + 1 : 2 * lat + 2] + jnp.sum(
                latent * (2.0 * e[lat : 2 * lat] + quad), axis=0, keepdims=True
            )
            var = jnp.maximum(var, 0.0) + 1e-05
            at[i] = jnp.concatenate(
                [
                    latent,
                    latent,
                    mask,
                    mask,
                    lax.rsqrt(var),
                    1e-06 * var,
                    jnp.zeros((64 - 2 * lat - 4, var.shape[1]), F32),
                ],
                axis=0,
            )

    def columns(j):
        piece = at[j // 4, :, pl.ds(pl.multiple_of((j % 4) * span, span), span)]
        a = piece.T
        return a.astype(BF), a[:, 2 * lat + 2 : 2 * lat + 3], a[:, 2 * lat + 3 : 2 * lat + 4]

    def unit(u, eps):
        return u * lax.rsqrt(jnp.mean(u * u, axis=1, keepdims=True) + eps)

    own = (block // 2 + 1) * 4 + block % 2 + 1
    a, _, eps = columns(own)
    uq = nn(a, rq_ref[...])
    raw = jnp.where(block % 2 == 0, qa_ref[0].astype(F32), qb_ref[0].astype(F32))
    uq = uq + raw
    queries = []
    for h in range(heads):
        q = unit(uq[:, h * 128 : (h + 1) * 128], eps) * scale_ref[h]
        queries.append(q.astype(BF))

    num[...] = jnp.zeros_like(num)
    den[...] = jnp.zeros_like(den)

    def one(i, _):
        j = slot_ref[block * slots + i]

        @pl.when(j >= 0)
        def _():
            @pl.when(need[j] == 1)
            def _():
                need[j] = 2
                pltpu.make_async_copy(ka.at[0], pk.at[j], sem.at[0, j]).wait()
                pltpu.make_async_copy(va.at[0], pv.at[j], sem.at[1, j]).wait()
                a, rs, eps = columns(true_ref[j])
                uk = nn(a, rk_ref[...]) + pk[j].astype(F32)
                for h in range(heads):
                    cut = slice(h * 128, (h + 1) * 128)
                    pk[j, :, cut] = unit(uk[:, cut], eps).astype(BF)
                uv = (nn(a, rv_ref[...]) + pv[j].astype(F32)) * rs
                pv[j] = uv.astype(BF)

            for h in range(heads):
                cut = slice(h * 128, (h + 1) * 128)
                w = jnp.exp(nt(queries[h], pk[j, :, cut]))
                den[h] += jnp.broadcast_to(jnp.sum(w, axis=1, keepdims=True), (span, 128))
                num[:, cut] += nn(w.astype(BF), pv[j, :, cut])

        return 0

    lax.fori_loop(0, slots, one, 0)
    for h in range(heads):
        cut = slice(h * 128, (h + 1) * 128)
        o_ref[0, :, cut] = (num[:, cut] / den[h]).astype(BF)


def shift(values, axis, by):
    count = lax.axis_size(axis)
    if by > 0:
        return lax.ppermute(values, axis, [(i, i + 1) for i in range(count - 1)])
    return lax.ppermute(values, axis, [(i + 1, i) for i in range(count - 1)])


def swap(values, axis, bit):
    count = lax.axis_size(axis)
    return lax.ppermute(values, axis, [(i, i ^ bit) for i in range(count)])


def per_device(
    features,
    norm_gain,
    norm_bias,
    latent_kernel,
    latent_bias,
    token_mask,
    embed_weight,
    mask_token,
    pos_embed,
    query_weight,
    key_weight,
    value_weight,
    logit_scale,
    pattern,
):
    frames, slab_rows, row_width, channels = features.shape
    per_group = channels // GROUPS
    time_count = lax.axis_size("tm")
    row_count = lax.axis_size("row")
    time_index = lax.axis_index("tm")
    row_index = lax.axis_index("row")
    tokens = frames * slab_rows * row_width
    latents, width = embed_weight.shape
    heads = logit_scale.shape[0]
    inner = query_weight.shape[1]
    row_pairs = slab_rows // 2
    span = 2 * row_width
    blocks = frames * row_pairs
    slots = pattern.shape[-1]
    cell_count = frames * time_count * slab_rows * row_count * row_width * per_group

    flat = features.reshape(tokens, channels)
    sums = pl.pallas_call(
        stats_kernel,
        out_shape=jax.ShapeDtypeStruct((2, channels), F32),
        grid=(4,),
        in_specs=[pl.BlockSpec((tokens // 4, channels), lambda i: (i, 0))],
        out_specs=pl.BlockSpec((2, channels), lambda i: (0, 0)),
        compiler_params=params(),
    )(flat)
    for axis, count in (("row", row_count), ("tm", time_count)):
        bit = 1
        while bit < count:
            sums = sums + swap(sums, axis, bit)
            bit *= 2

    pos = pos_embed.reshape(tokens, width)
    side, mp, aug, am, gram = pl.pallas_call(
        side_kernel,
        out_shape=(
            jax.ShapeDtypeStruct((EXT - latents, tokens), F32),
            jax.ShapeDtypeStruct((tokens, 128), F32),
            jax.ShapeDtypeStruct((AUG, width), BF),
            jax.ShapeDtypeStruct((AUG, 128), F32),
            jax.ShapeDtypeStruct((latents, 128), F32),
        ),
        in_specs=[VM] * 4,
        out_specs=(VM,) * 5,
        scratch_shapes=[pltpu.VMEM((128, width), F32)],
        compiler_params=params(),
    )(pos, embed_weight, mask_token.reshape(1, -1), token_mask.reshape(1, -1))

    ka, kb, rk = project(pos, aug, mp, am, key_weight, frames, span)
    va, vb, rv = project(pos, aug, mp, am, value_weight, frames, span)
    qa, qb, rq = project(pos, aug, mp, am, query_weight, frames, span)

    even = row_index % 2 == 0

    def spread(first, second):
        up = shift(second, "row", 1)
        down = shift(first, "row", -1)
        outer = jnp.where(even, up, down)
        ahead = jnp.stack([first[-1], second[-1], outer[-1]])
        behind = jnp.stack([first[0], second[0], outer[0]])
        fwd = shift(ahead, "tm", 1)
        back = shift(behind, "tm", -1)
        corner = jnp.stack([jnp.where(even, fwd[1], fwd[0]), jnp.where(even, back[1], back[0])])
        return up, down, fwd, back, swap(corner, "row", 1)

    ku, kd, kf, kz, kc = spread(ka, kb)
    vu, vd, vf, vz, vc = spread(va, vb)

    taps = latent_kernel.transpose(3, 2, 1, 0, 4).reshape(27 * latents, channels)
    reach = (slab_rows + 4) * row_width
    local = pl.pallas_call(
        functools.partial(conv_kernel, count=cell_count, per_group=per_group, width=row_width),
        out_shape=jax.ShapeDtypeStruct((frames + 2, EXT, reach), F32),
        in_specs=[VM] * 6,
        out_specs=VM,
        compiler_params=params(),
    )(sums, norm_gain.reshape(1, -1), norm_bias.reshape(1, -1), flat, taps, side)
    half = reach // 2
    upper = shift(local[:, :, half:], "row", 1)
    lower = shift(local[:, :, :half], "row", -1)
    spread_rows = local + jnp.concatenate([upper, lower], axis=-1)
    fore = shift(spread_rows[frames:], "tm", 1)
    aft = shift(spread_rows[:2], "tm", -1)

    pair_total = row_pairs * row_count
    listed = pattern.reshape(blocks, slots)
    clamped = jnp.maximum(listed, 0)
    key_frame = clamped // pair_total - time_index * frames + 1
    key_pair = clamped % pair_total - row_index * row_pairs + 1
    across = (key_frame == 0) | (key_frame == frames + 1)
    edge = (key_pair == 0) | (key_pair == 3)
    place = jnp.where(across & edge & ~even, 3 - key_pair, key_pair)
    slot = jnp.where(listed >= 0, key_frame * 4 + place, -1).reshape(-1)
    ids = jnp.arange((frames + 2) * 4)
    id_frame, id_pair = ids // 4, ids % 4
    flip = ((id_frame == 0) | (id_frame == frames + 1)) & ((id_pair == 0) | (id_pair == 3)) & ~even
    true_id = jnp.where(flip, id_frame * 4 + 3 - id_pair, ids)
    total = (frames + 2) * 4

    out = pl.pallas_call(
        functools.partial(attend_kernel, slots=slots),
        out_shape=jax.ShapeDtypeStruct((blocks, span, inner), BF),
        grid_spec=pltpu.PrefetchScalarGridSpec(
            num_scalar_prefetch=3,
            grid=(blocks,),
            in_specs=[VM] * 8
            + [pl.BlockSpec((1, span, inner), lambda b, *_: (b // 2, 0, 0))] * 2
            + [ANY] * 14,
            out_specs=pl.BlockSpec((1, span, inner), lambda b, *_: (b, 0, 0)),
            scratch_shapes=[
                pltpu.VMEM((total, span, inner), BF),
                pltpu.VMEM((total, span, inner), BF),
                pltpu.VMEM((frames + 2, 64, reach), F32),
                pltpu.VMEM((span, inner), F32),
                pltpu.VMEM((heads, span, 128), F32),
                pltpu.SMEM((total,), jnp.int32),
                pltpu.SemaphoreType.DMA((2, total)),
            ],
        ),
        compiler_params=params(),
    )(
        slot, true_id, logit_scale / (inner // heads),
        spread_rows, fore, aft, latent_bias.reshape(-1, 1), gram, rk, rv, rq, qa, qb,
        ka, kb, va, vb, ku, kd, vu, vd, kf, kz, vf, vz, kc, vc,
    )
    return out.reshape(frames, slab_rows, row_width, inner)


def solution(mesh):
    in_specs = (
        P("tm", "row", None, None),
        P(),
        P(),
        P(),
        P(),
        P("tm", "row", None),
        P(),
        P(),
        P("tm", "row", None, None),
        P(),
        P(),
        P(),
        P(),
        P("tm", "row", None),
    )
    out_specs = P("tm", "row", None, None)
    return jax.shard_map(
        per_device, mesh=mesh, in_specs=in_specs, out_specs=out_specs, check_vma=False
    )
```

```python
import functools

import jax
import jax.numpy as jnp
from jax import lax
from jax.experimental import pallas as pl
from jax.experimental.pallas import tpu as pltpu
from jax.sharding import PartitionSpec as P

GROUPS = 32
BF = jnp.bfloat16
F32 = jnp.float32
VM = pl.BlockSpec(memory_space=pltpu.VMEM)
SM = pl.BlockSpec(memory_space=pltpu.SMEM)
ANY = pl.BlockSpec(memory_space=pl.ANY)
HBM = pl.BlockSpec(memory_space=pltpu.HBM)
AUG = 32
ONES = 19
EXT = 40
MIB = 1 << 20


def params(mib):
    return pltpu.CompilerParams(vmem_limit_bytes=mib * MIB)


def nt(a, b):
    return lax.dot_general(a, b, (((1,), (1,)), ((), ())), preferred_element_type=F32)


def nn(a, b):
    return lax.dot_general(a, b, (((1,), (0,)), ((), ())), preferred_element_type=F32)


def stats_kernel(x_ref, o_ref):
    @pl.when(pl.program_id(0) == 0)
    def _():
        o_ref[...] = jnp.zeros_like(o_ref)

    x = x_ref[...].astype(F32)
    o_ref[0:1] += jnp.sum(x, axis=0, keepdims=True)
    o_ref[1:2] += jnp.sum(x * x, axis=0, keepdims=True)


def fetch_rows(pos_ref, x, sem, pieces):
    rows = pos_ref.shape[0] // pieces
    return [
        pltpu.make_async_copy(
            pos_ref.at[pl.ds(i * rows, rows)], x.at[pl.ds(i * rows, rows)], sem.at[i]
        )
        for i in range(pieces)
    ]


def project_tile(x, mp, am, w_ref, a_ref, b_ref, r_ref, first, last, arrive):
    lat = 16
    frames, span, tile = a_ref.shape
    tokens = x.shape[0] - AUG
    aw = nn(x[pl.ds(tokens, AUG)], w_ref[...])
    colsum = aw[ONES : ONES + 1]
    ew = aw[0:lat] - am[0:lat, 0:1] * colsum
    mw = jnp.sum(aw[lat : lat + 3], axis=0, keepdims=True)
    mean_m = jnp.sum(am[lat : lat + 3, 0:1], axis=0, keepdims=True)
    mw = mw - mean_m * colsum
    ewh = ew.astype(BF).astype(F32)
    mwh = mw.astype(BF).astype(F32)
    r_ref[0:lat] = ewh.astype(BF)
    r_ref[lat : 2 * lat] = (ew - ewh).astype(BF)
    r_ref[2 * lat : 4 * lat] = jnp.concatenate(
        [mwh, mw - mwh, jnp.zeros((2 * lat - 2, mw.shape[1]), F32)], axis=0
    ).astype(BF)
    for f in range(frames):
        rows = slice(2 * f * span, (2 * f + 2) * span)
        arrive(f, rows)
        acc = nn(x[rows], w_ref[...])
        for k in range(tile // 128):
            part = (acc[:, cut(k)] - mp[rows] * colsum[:, cut(k)]).astype(BF)
            a_ref[f, :, cut(k)] = part[0:span]
            b_ref[f, :, cut(k)] = part[span:]
            edge = {0: first, frames - 1: last}.get(f)
            if edge is not None:
                edge[0, :, cut(k)] = part[0:span]
                edge[1, :, cut(k)] = part[span:]


def front_kernel(pos_ref, embed_ref, mtok_ref, mask_ref, w_ref, a_ref, b_ref, e_ref, l_ref, r_ref,
                 side_ref, c_ref, aug_ref, mp_ref, am_ref, x, aug, sem):
    tokens = pos_ref.shape[0]
    lat, width = embed_ref.shape
    pieces = sem.shape[0]

    @pl.when(pl.program_id(0) == 0)
    def _():
        copies = fetch_rows(pos_ref, x, sem, pieces)
        for copy in copies:
            copy.start()
        aug[...] = jnp.zeros_like(aug)
        aug[0:lat] = embed_ref[...].astype(F32)
        m = mtok_ref[...]
        hi = m.astype(BF).astype(F32)
        mid = (m - hi).astype(BF).astype(F32)
        low = (m - hi - mid).astype(BF).astype(F32)
        aug[lat : lat + 1] = hi
        aug[lat + 1 : lat + 2] = mid
        aug[lat + 2 : lat + 3] = low
        aug[ONES : ONES + 1] = jnp.ones_like(hi)
        rows = aug[...].astype(BF)
        x[pl.ds(tokens, AUG), :] = rows[0:AUG]
        aug_ref[...] = rows[0:AUG]
        gram = nt(rows, rows) * (1.0 / width)
        am_ref[...] = jnp.broadcast_to(gram[0:AUG, ONES : ONES + 1], am_ref.shape)
        mean_e = gram[0:lat, ONES : ONES + 1]
        mean_m = jnp.sum(gram[lat : lat + 3, ONES : ONES + 1], axis=0, keepdims=True)
        c_ref[...] = gram[0:lat] - mean_e * gram[ONES : ONES + 1]
        mrow = jnp.sum(gram[lat : lat + 3], axis=0, keepdims=True)
        cm = jnp.sum(mrow[:, lat : lat + 3], axis=1, keepdims=True) - mean_m * mean_m
        def arrive(i, span):
            copies[i].wait()
            d = nt(x[span], rows) * (1.0 / width)
            mp_ref[span] = jnp.broadcast_to(d[:, ONES : ONES + 1], d.shape)
            sq = jnp.zeros(d.shape, F32)
            for k in range(width // 128):
                p = x[span, k * 128 : (k + 1) * 128].astype(F32)
                sq = sq + p * p
            dt = d.T
            mean_pos = dt[ONES : ONES + 1]
            vp = jnp.sum(sq.T, axis=0, keepdims=True) * (1.0 / width) - mean_pos * mean_pos
            g = dt[0:lat] - mean_e * mean_pos
            gm = jnp.sum(dt[lat : lat + 3], axis=0, keepdims=True) - mean_m * mean_pos
            masked = mask_ref[:, span] == 1
            side_ref[0:lat, span] = jnp.where(masked, 0.0, g)
            side_ref[lat : lat + 8, span] = jnp.concatenate(
                [
                    masked.astype(F32),
                    jnp.where(masked, vp + 2.0 * gm + cm, vp),
                    jnp.zeros((6, g.shape[1]), F32),
                ],
                axis=0,
            )

        project_tile(x, mp_ref, am_ref, w_ref, a_ref, b_ref, r_ref, e_ref, l_ref, arrive)

    @pl.when(pl.program_id(0) > 0)
    def _():
        stay = lambda i, rows: None
        project_tile(x, mp_ref, am_ref, w_ref, a_ref, b_ref, r_ref, e_ref, l_ref, stay)


def value_kernel(pos_ref, aug_ref, mp_ref, am_ref, w_ref, _0, _1, a, b, e, l, r, x, sem):
    proj_kernel(pos_ref, aug_ref, mp_ref, am_ref, w_ref, a, b, r, x, sem, e, l)


def proj_kernel(
    pos_ref, aug_ref, mp_ref, am_ref, w_ref, a_ref, b_ref, r_ref, x, sem, first=None, last=None
):
    tokens = pos_ref.shape[0]
    rest = (x, mp_ref, am_ref, w_ref, a_ref, b_ref, r_ref, first, last)

    @pl.when(pl.program_id(0) == 0)
    def _():
        copies = fetch_rows(pos_ref, x, sem, sem.shape[0])
        for copy in copies:
            copy.start()
        x[pl.ds(tokens, AUG), :] = aug_ref[...]
        project_tile(*rest, lambda i, rows: copies[i].wait())

    @pl.when(pl.program_id(0) > 0)
    def _():
        project_tile(*rest, lambda i, rows: None)


def project(kind, pos, extra, weight, frames, span, into=()):
    tokens, width = pos.shape
    inner = weight.shape[1]
    tile = 256
    steps = inner // tile
    double = kind != "query"
    skip = steps if kind == "value" else 0
    cols = 2 * inner if double else inner
    shapes = (jax.ShapeDtypeStruct((frames, span, inner), BF),) * 2
    specs = (pl.BlockSpec((frames, span, tile), lambda n: (0, 0, n)),) * 2
    if double:
        shapes += (jax.ShapeDtypeStruct((2, span, cols), BF),) * 2
        specs += (pl.BlockSpec((2, span, tile), lambda n: (0, 0, n + skip)),) * 2
    shapes += (jax.ShapeDtypeStruct((64, inner), BF),)
    specs += (pl.BlockSpec((64, tile), lambda n: (0, n)),)
    scratch = [pltpu.VMEM((tokens + AUG, width), BF)]
    pieces = frames
    if kind == "key":
        shapes += (
            jax.ShapeDtypeStruct((EXT - 16, tokens), F32),
            jax.ShapeDtypeStruct((16, 128), F32),
            jax.ShapeDtypeStruct((AUG, width), BF),
            jax.ShapeDtypeStruct((tokens, 128), F32),
            jax.ShapeDtypeStruct((AUG, 128), F32),
        )
        specs += (VM,) * 5
        scratch.append(pltpu.VMEM((128, width), F32))
    scratch.append(pltpu.SemaphoreType.DMA((pieces,)))
    kernel = {"key": front_kernel, "value": value_kernel, "query": proj_kernel}[kind]
    return pl.pallas_call(
        kernel,
        out_shape=shapes,
        grid=(steps,),
        in_specs=[HBM, VM, VM, VM, pl.BlockSpec((width, tile), lambda n: (0, n))]
        + [ANY] * len(into),
        out_specs=specs,
        scratch_shapes=scratch,
        input_output_aliases={5 + i: 2 + i for i in range(len(into))},
        compiler_params=params(24),
        cost_estimate=pl.CostEstimate(
            flops=2 * tokens * width * inner, bytes_accessed=12 * MIB, transcendentals=0
        ),
    )(pos, *extra, weight, *into)


def conv_kernel(sum_ref, gain_ref, bias_ref, x_ref, k_ref, side_ref, o_ref, *, count, per_group, width):
    sums = sum_ref[...]
    channels = sums.shape[1]
    lane = lax.broadcasted_iota(jnp.int32, sums.shape, 1)
    step = 1
    while step < per_group:
        sums = sums + jnp.where(
            (lane & step) == 0, pltpu.roll(sums, channels - step, 1), pltpu.roll(sums, step, 1)
        )
        step *= 2
    average = sums[0:1] * (1.0 / count)
    variance = sums[1:2] * (1.0 / count) - average * average
    inverse = lax.rsqrt(variance + 1e-06)
    scale = inverse * gain_ref[...]
    shift = bias_ref[...] - average * scale
    frames = o_ref.shape[0] - 2
    lat = 16
    cells = x_ref.shape[0] // frames
    o_ref[...] = jnp.zeros_like(o_ref)
    pad = (o_ref.shape[2] - cells) // 2
    w = lax.broadcasted_iota(jnp.int32, (9 * lat, cells), 1) % width
    acc = [None] * (frames + 2)
    for f in range(frames):
        v = x_ref[f * cells : (f + 1) * cells].astype(F32) * scale + shift
        act = (v / (1.0 + jnp.exp(-v))).astype(BF)
        y = nt(k_ref[...], act)
        n = 9 * lat
        y = (
            y[n : 2 * n]
            + jnp.where(w == 0, 0.0, pltpu.roll(y[0:n], 1, 1))
            + jnp.where(w == width - 1, 0.0, pltpu.roll(y[2 * n : 3 * n], cells - 1, 1))
        )
        gap = jnp.zeros((3 * lat, pad), F32)
        m = 3 * lat
        z = [jnp.concatenate([gap, y[b * m : (b + 1) * m], gap], axis=1) for b in range(3)]
        full = z[0].shape[1]
        z = z[1] + pltpu.roll(z[0], width, 1) + pltpu.roll(z[2], full - width, 1)
        for a in range(3):
            part = z[a * lat : (a + 1) * lat]
            i = f - a + 2
            acc[i] = part if acc[i] is None else acc[i] + part
        o_ref[f + 1, lat:EXT, pad : pad + cells] = side_ref[:, f * cells : (f + 1) * cells]
    for i in range(frames + 2):
        o_ref[i, 0:lat] = acc[i]


def columns_of(at, j, span):
    lat = 16
    piece = at[j // 4, :, pl.ds(pl.multiple_of((j % 4) * span, span), span)]
    a = piece.T
    return a.astype(BF), a[:, 2 * lat + 2 : 2 * lat + 3], a[:, 2 * lat + 3 : 2 * lat + 4]


def unit(u, eps):
    return u * lax.rsqrt(jnp.mean(u * u, axis=1, keepdims=True) + eps)


def cut(h):
    return slice(h * 128, (h + 1) * 128)


def finish_block(j, i, at, rk_ref, rv_ref, k, v, pk, pv):
    a, rs, eps = columns_of(at, j, pk.shape[1])
    uk = nn(a, rk_ref[...]) + k.astype(F32)
    uv = (nn(a, rv_ref[...]) + v.astype(F32)) * rs
    for h in range(uk.shape[1] // 128):
        pk[i, :, cut(h)] = unit(uk[:, cut(h)], eps).astype(BF)
    pv[i] = uv.astype(BF)


def attend_block(q, pk, pv, i, num, den):
    heads = q.shape[1] // 128
    scores = [nt(q[:, cut(h)], pk[i, :, cut(h)]) for h in range(heads)]
    weights = [jnp.exp(s) for s in scores]
    sums = [nn(w.astype(BF), pv[i, :, cut(h)]) for h, w in enumerate(weights)]
    for h in range(heads):
        den[h] += weights[h]
        num[:, cut(h)] += sums[h]


def near_kernel(
    slot_ref, scale_ref,
    s_ref, up_ref, low_ref, bias_ref, c_ref, rk_ref, rv_ref, rq_ref, qa_ref, qb_ref,
    ka, kb, va, vb,
    q_ref, n_ref, d_ref, at, pk, pv, num, den, ready, *, slots,
):
    block = pl.program_id(0)
    frames = ka.shape[0]
    span = pk.shape[1]
    inner = pk.shape[2]
    heads = inner // 128
    lat = 16

    @pl.when(block == 0)
    def _():
        for j in range(ready.shape[0]):
            ready[j] = 0
        c = c_ref[:, 0:lat]
        ch = c.astype(BF)
        cl = (c - ch.astype(F32)).astype(BF)
        for i in range(frames + 2):
            e = s_ref[i] + jnp.concatenate([up_ref[i], low_ref[i]], axis=1)
            mask = e[2 * lat : 2 * lat + 1]
            latent = (e[0:lat] + bias_ref[...]).astype(BF).astype(F32)
            latent = jnp.where(mask > 0.5, 0.0, latent)
            lb = latent.astype(BF)
            quad = nn(ch, lb) + nn(cl, lb)
            var = e[2 * lat + 1 : 2 * lat + 2] + jnp.sum(
                latent * (2.0 * e[lat : 2 * lat] + quad), axis=0, keepdims=True
            )
            var = jnp.maximum(var, 0.0) + 1e-05
            at[i] = jnp.concatenate(
                [
                    latent,
                    latent,
                    mask,
                    mask,
                    lax.rsqrt(var),
                    1e-06 * var,
                    jnp.zeros((64 - 2 * lat - 4, var.shape[1]), F32),
                ],
                axis=0,
            )

    own = (block // 2 + 1) * 4 + block % 2 + 1
    a, _, eps = columns_of(at, own, span)
    uq = nn(a, rq_ref[...])
    uq = uq + jnp.where(block % 2 == 0, qa_ref[0].astype(F32), qb_ref[0].astype(F32))
    for h in range(heads):
        q_ref[0, :, cut(h)] = (unit(uq[:, cut(h)], eps) * scale_ref[h]).astype(BF)
    num[...] = jnp.zeros_like(num)
    den[...] = jnp.zeros_like(den)

    def one(i, _):
        j = slot_ref[block * slots + i]
        f, p = j // 4 - 1, j % 4 - 1

        @pl.when((j >= 0) & (f >= 0) & (f < frames) & (p >= 0) & (p < 2))
        def _():
            n = f * 2 + p

            @pl.when(ready[n] == 0)
            def _():
                ready[n] = 1

                @pl.when(p == 0)
                def _():
                    finish_block(j, n, at, rk_ref, rv_ref, ka[f], va[f], pk, pv)

                @pl.when(p == 1)
                def _():
                    finish_block(j, n, at, rk_ref, rv_ref, kb[f], vb[f], pk, pv)

            attend_block(q_ref[0], pk, pv, n, num, den)

        return 0

    lax.fori_loop(0, slots, one, 0)
    n_ref[0] = num[...]
    d_ref[0] = jnp.concatenate(
        [jnp.sum(den[h], axis=1, keepdims=True) for h in range(heads)], axis=1
    )


def far_kernel(
    slot_ref, true_ref,
    q_ref, n_ref, d_ref, at, rk_ref, rv_ref, ku, kd, vu, vd, kf, kz, kg, kh, kc,
    o_ref, raw, pk, pv, num, den, need, sem, *, slots,
):
    block = pl.program_id(0)
    frames = ku.shape[0]
    inner = pk.shape[2]
    heads = inner // 128
    total = pk.shape[0]

    def local(j):
        return 0 <= j // 4 - 1 < frames and 1 <= j % 4 <= 2

    def source(j):
        f, q = j // 4 - 1, j % 4
        late = f >= 0
        if q == 3:
            return kc.at[int(late)]
        if q == 0:
            return (kh if late else kg).at[0]
        return (kz if late else kf).at[q - 1]

    @pl.when(block == 0)
    def _():
        for j in range(total):
            need[j] = 0

        def mark(i, _):
            j = slot_ref[i]

            @pl.when(j >= 0)
            def _():
                need[j] = 1

            return 0

        lax.fori_loop(0, slot_ref.shape[0], mark, 0)
        for j in range(total):
            if local(j):
                continue

            @pl.when(need[j] == 1)
            def _(j=j):
                f = j // 4 - 1
                if 0 <= f < frames:
                    k, v = (kd, vd) if j % 4 else (ku, vu)
                    pltpu.make_async_copy(k.at[f], raw.at[j, :, 0:inner], sem.at[j]).start()
                    pltpu.make_async_copy(v.at[f], raw.at[j, :, inner:], sem.at[j]).start()
                else:
                    pltpu.make_async_copy(source(j), raw.at[j], sem.at[j]).start()

    num[...] = n_ref[0]
    den[...] = jnp.zeros_like(den)

    def one(i, _):
        j = slot_ref[block * slots + i]
        f, p = j // 4 - 1, j % 4 - 1
        inside = (f >= 0) & (f < frames) & (p >= 0) & (p < 2)

        @pl.when((j >= 0) & ~inside)
        def _():
            @pl.when(need[j] == 1)
            def _():
                need[j] = 2
                pltpu.make_async_copy(kf.at[0], raw.at[j], sem.at[j]).wait()
                k, v = raw[j, :, 0:inner], raw[j, :, inner:]
                finish_block(true_ref[j], j, at, rk_ref, rv_ref, k, v, pk, pv)

            attend_block(q_ref[0], pk, pv, j, num, den)

        return 0

    lax.fori_loop(0, slots, one, 0)
    for h in range(heads):
        whole = d_ref[0, :, h : h + 1] + jnp.sum(den[h], axis=1, keepdims=True)
        o_ref[0, :, cut(h)] = (num[:, cut(h)] / whole).astype(BF)


def shift(values, axis, by):
    count = lax.axis_size(axis)
    if by > 0:
        return lax.ppermute(values, axis, [(i, i + 1) for i in range(count - 1)])
    return lax.ppermute(values, axis, [(i + 1, i) for i in range(count - 1)])


def swap(values, axis, bit):
    count = lax.axis_size(axis)
    return lax.ppermute(values, axis, [(i, i ^ bit) for i in range(count)])


def per_device(
    features,
    norm_gain,
    norm_bias,
    latent_kernel,
    latent_bias,
    token_mask,
    embed_weight,
    mask_token,
    pos_embed,
    query_weight,
    key_weight,
    value_weight,
    logit_scale,
    pattern,
):
    frames, slab_rows, row_width, channels = features.shape
    per_group = channels // GROUPS
    time_count = lax.axis_size("tm")
    row_count = lax.axis_size("row")
    time_index = lax.axis_index("tm")
    row_index = lax.axis_index("row")
    tokens = frames * slab_rows * row_width
    latents, width = embed_weight.shape
    heads = logit_scale.shape[0]
    inner = query_weight.shape[1]
    row_pairs = slab_rows // 2
    span = 2 * row_width
    blocks = frames * row_pairs
    slots = pattern.shape[-1]
    cell_count = frames * time_count * slab_rows * row_count * row_width * per_group

    flat = features.reshape(tokens, channels)
    sums = pl.pallas_call(
        stats_kernel,
        out_shape=jax.ShapeDtypeStruct((2, channels), F32),
        grid=(4,),
        in_specs=[pl.BlockSpec((tokens // 4, channels), lambda i: (i, 0))],
        out_specs=pl.BlockSpec((2, channels), lambda i: (0, 0)),
        compiler_params=params(4),
    )(flat)
    rounds = []
    bit = 2
    while bit < row_count:
        rounds.append(("row", bit))
        bit *= 2
    apart = len(rounds)
    rounds.append(("row", 1))
    bit = 1
    while bit < time_count:
        rounds.append(("tm", bit))
        bit *= 2
    def after(value, *others):
        return lax.optimization_barrier((value, *others))[0]

    def advance(value, step):
        axis, bit = rounds[step]
        return value + swap(value, axis, bit)

    steps = [sums]
    for step in range(len(rounds)):
        steps.append(advance(steps[-1], step))
    sums = steps[-1]
    near_done = steps[apart + 1]
    hbm = lambda x: pltpu.with_memory_space_constraint(x, pltpu.HBM)
    pos = hbm(pos_embed.reshape(tokens, width))
    front = project(
        "key", pos,
        (after(embed_weight, near_done), mask_token.reshape(1, -1), token_mask.reshape(1, -1)),
        hbm(key_weight), frames, span,
    )
    ka, kb = front[:2]
    rk, side, gram = front[4:7]
    extra = front[7:]
    up_k = shift(after(kb, steps[apart + 2]), "row", 1)
    down_k = shift(after(ka, steps[apart + 2]), "row", -1)
    taps = latent_kernel.transpose(3, 2, 1, 0, 4).reshape(27 * latents, channels)
    reach = (slab_rows + 4) * row_width
    local = pl.pallas_call(
        functools.partial(conv_kernel, count=cell_count, per_group=per_group, width=row_width),
        out_shape=jax.ShapeDtypeStruct((frames + 2, EXT, reach), F32),
        in_specs=[VM] * 6,
        out_specs=VM,
        compiler_params=params(14),
    )(sums, norm_gain.reshape(1, -1), norm_bias.reshape(1, -1), flat, taps, side)
    fore = shift(local[frames:], "tm", 1)
    aft = shift(local[:2], "tm", -1)
    blank = jnp.zeros((frames - 2, *local.shape[1:]), F32)
    tall = local + jnp.concatenate([fore, blank, aft], axis=0)
    half = reach // 2
    upper = shift(tall[:, :, half:], "row", 1)
    lower = shift(tall[:, :, :half], "row", -1)
    va, vb, edge, last, rv = project(
        "value", pos, (after(extra[0], fore, aft), *extra[1:]), hbm(value_weight), frames,
        span, front[2:4],
    )
    qa, qb, rq = project(
        "query", pos, (after(extra[0], va), *extra[1:]), hbm(query_weight), frames, span
    )
    fwd = shift(after(last, fore, aft), "tm", 1)
    back = shift(after(edge, fore, aft), "tm", -1)
    up_v = shift(after(vb, upper, lower), "row", 1)
    down_v = shift(after(va, upper, lower), "row", -1)
    even = row_index % 2 == 0

    pair_total = row_pairs * row_count
    listed = pattern.reshape(blocks, slots)
    clamped = jnp.maximum(listed, 0)
    key_frame = clamped // pair_total - time_index * frames + 1
    key_pair = clamped % pair_total - row_index * row_pairs + 1
    across = (key_frame == 0) | (key_frame == frames + 1)
    edge = (key_pair == 0) | (key_pair == 3)
    place = jnp.where(across & edge & ~even, 3 - key_pair, key_pair)
    slot = jnp.where(listed >= 0, key_frame * 4 + place, -1).reshape(-1)
    ids = jnp.arange((frames + 2) * 4)
    id_frame, id_pair = ids // 4, ids % 4
    flip = ((id_frame == 0) | (id_frame == frames + 1)) & ((id_pair == 0) | (id_pair == 3)) & ~even
    true_id = jnp.where(flip, id_frame * 4 + 3 - id_pair, ids)
    total = (frames + 2) * 4

    each = lambda b, *_: (b, 0, 0)
    half_block = pl.BlockSpec((1, span, inner), lambda b, *_: (b // 2, 0, 0))
    whole_block = pl.BlockSpec((1, span, inner), each)
    den_block = pl.BlockSpec((1, span, heads), each)
    query, num, den, cols = pl.pallas_call(
        functools.partial(near_kernel, slots=slots),
        out_shape=(
            jax.ShapeDtypeStruct((blocks, span, inner), BF),
            jax.ShapeDtypeStruct((blocks, span, inner), F32),
            jax.ShapeDtypeStruct((blocks, span, heads), F32),
            jax.ShapeDtypeStruct((frames + 2, 64, reach), F32),
        ),
        grid_spec=pltpu.PrefetchScalarGridSpec(
            num_scalar_prefetch=2,
            grid=(blocks,),
            in_specs=[VM] * 8 + [half_block] * 2 + [VM] * 4,
            out_specs=(whole_block, whole_block, den_block, VM),
            scratch_shapes=[
                pltpu.VMEM((blocks, span, inner), BF),
                pltpu.VMEM((blocks, span, inner), BF),
                pltpu.VMEM((span, inner), F32),
                pltpu.VMEM((heads, span, 128), F32),
                pltpu.SMEM((blocks,), jnp.int32),
            ],
        ),
        compiler_params=params(26),
        cost_estimate=pl.CostEstimate(flops=16 * 10**9, bytes_accessed=16 * MIB, transcendentals=0),
    )(
        slot, logit_scale / (inner // heads),
        tall, upper, lower, latent_bias.reshape(-1, 1), gram, rk, rv, rq, qa, qb,
        ka, kb, va, vb,
    )
    up_k, up_v = after(up_k, num), after(up_v, num)
    def outer(i):
        pick = lambda u, d: jnp.where(even, u[i], d[i])
        return jnp.concatenate([pick(up_k, down_k), pick(up_v, down_v)], axis=-1)[None]

    outer_fwd = shift(outer(-1), "tm", 1)
    outer_back = shift(outer(0), "tm", -1)
    corner = jnp.stack([jnp.where(even, fwd[1], fwd[0]), jnp.where(even, back[1], back[0])])
    corner = swap(corner, "row", 1)

    out = pl.pallas_call(
        functools.partial(far_kernel, slots=slots),
        out_shape=jax.ShapeDtypeStruct((blocks, span, inner), BF),
        grid_spec=pltpu.PrefetchScalarGridSpec(
            num_scalar_prefetch=2,
            grid=(blocks,),
            in_specs=[whole_block, whole_block, den_block, VM, VM, VM] + [ANY] * 9,
            out_specs=whole_block,
            scratch_shapes=[
                pltpu.VMEM((total, span, 2 * inner), BF),
                pltpu.VMEM((total, span, inner), BF),
                pltpu.VMEM((total, span, inner), BF),
                pltpu.VMEM((span, inner), F32),
                pltpu.VMEM((heads, span, 128), F32),
                pltpu.SMEM((total,), jnp.int32),
                pltpu.SemaphoreType.DMA((total,)),
            ],
        ),
        compiler_params=params(38),
    )(
        slot, true_id, query, num, den, cols, rk, rv,
        up_k, down_k, up_v, down_v, fwd, back, outer_fwd, outer_back, corner,
    )
    return out.reshape(frames, slab_rows, row_width, inner)


def solution(mesh):
    in_specs = (
        P("tm", "row", None, None),
        P(),
        P(),
        P(),
        P(),
        P("tm", "row", None),
        P(),
        P(),
        P("tm", "row", None, None),
        P(),
        P(),
        P(),
        P(),
        P("tm", "row", None),
    )
    out_specs = P("tm", "row", None, None)
    return jax.shard_map(
        per_device, mesh=mesh, in_specs=in_specs, out_specs=out_specs, check_vma=False
    )
```

```python
import functools

import jax
import jax.numpy as jnp
from jax import lax
from jax.experimental import pallas as pl
from jax.experimental.pallas import tpu as pltpu
from jax.sharding import PartitionSpec as P


GROUPS = 32
BF = jnp.bfloat16
F32 = jnp.float32
VM = pl.BlockSpec(memory_space=pltpu.VMEM)
SM = pl.BlockSpec(memory_space=pltpu.SMEM)
ANY = pl.BlockSpec(memory_space=pl.ANY)
HBM = pl.BlockSpec(memory_space=pltpu.HBM)
AUG = 32
ONES = 19
EXT = 40
MIB = 1 << 20


def params(mib):
    return pltpu.CompilerParams(vmem_limit_bytes=mib * MIB)


def nt(a, b):
    return lax.dot_general(a, b, (((1,), (1,)), ((), ())), preferred_element_type=F32)


def nn(a, b):
    return lax.dot_general(a, b, (((1,), (0,)), ((), ())), preferred_element_type=F32)


def stats_kernel(x_ref, o_ref):
    @pl.when(pl.program_id(0) == 0)
    def _():
        o_ref[...] = jnp.zeros_like(o_ref)

    x = x_ref[...].astype(F32)
    o_ref[0:1] += jnp.sum(x, axis=0, keepdims=True)
    o_ref[1:2] += jnp.sum(x * x, axis=0, keepdims=True)


def fetch_rows(pos_ref, x, sem, pieces):
    rows = pos_ref.shape[0] // pieces
    return [
        pltpu.make_async_copy(
            pos_ref.at[pl.ds(i * rows, rows)], x.at[pl.ds(i * rows, rows)], sem.at[i]
        )
        for i in range(pieces)
    ]


def project_tile(x, mp, am, w_ref, a_ref, b_ref, r_ref, first, last, arrive):
    lat = 16
    frames, span, tile = a_ref.shape
    tokens = x.shape[0] - AUG
    aw = nn(x[pl.ds(tokens, AUG)], w_ref[...])
    colsum = aw[ONES : ONES + 1]
    ew = aw[0:lat] - am[0:lat, 0:1] * colsum
    mw = jnp.sum(aw[lat : lat + 3], axis=0, keepdims=True)
    mean_m = jnp.sum(am[lat : lat + 3, 0:1], axis=0, keepdims=True)
    mw = mw - mean_m * colsum
    ewh = ew.astype(BF).astype(F32)
    mwh = mw.astype(BF).astype(F32)
    r_ref[0:lat] = ewh.astype(BF)
    r_ref[lat : 2 * lat] = (ew - ewh).astype(BF)
    r_ref[2 * lat : 4 * lat] = jnp.concatenate(
        [mwh, mw - mwh, jnp.zeros((2 * lat - 2, mw.shape[1]), F32)], axis=0
    ).astype(BF)
    for f in range(frames):
        rows = slice(2 * f * span, (2 * f + 2) * span)
        arrive(f, rows)
        acc = nn(x[rows], w_ref[...])
        for k in range(tile // 128):
            part = (acc[:, cut(k)] - mp[rows] * colsum[:, cut(k)]).astype(BF)
            a_ref[f, :, cut(k)] = part[0:span]
            b_ref[f, :, cut(k)] = part[span:]
            edge = {0: first, frames - 1: last}.get(f)
            if edge is not None:
                edge[0, :, cut(k)] = part[0:span]
                edge[1, :, cut(k)] = part[span:]


def front_kernel(pos_ref, embed_ref, mtok_ref, mask_ref, w_ref, a_ref, b_ref, e_ref, l_ref, r_ref,
                 side_ref, c_ref, aug_ref, mp_ref, am_ref, x, aug, sem):
    tokens = pos_ref.shape[0]
    lat, width = embed_ref.shape
    pieces = sem.shape[0]

    @pl.when(pl.program_id(0) == 0)
    def _():
        copies = fetch_rows(pos_ref, x, sem, pieces)
        for copy in copies:
            copy.start()
        aug[...] = jnp.zeros_like(aug)
        aug[0:lat] = embed_ref[...].astype(F32)
        m = mtok_ref[...]
        hi = m.astype(BF).astype(F32)
        mid = (m - hi).astype(BF).astype(F32)
        low = (m - hi - mid).astype(BF).astype(F32)
        aug[lat : lat + 1] = hi
        aug[lat + 1 : lat + 2] = mid
        aug[lat + 2 : lat + 3] = low
        aug[ONES : ONES + 1] = jnp.ones_like(hi)
        rows = aug[...].astype(BF)
        x[pl.ds(tokens, AUG), :] = rows[0:AUG]
        aug_ref[...] = rows[0:AUG]
        gram = nt(rows, rows) * (1.0 / width)
        am_ref[...] = jnp.broadcast_to(gram[0:AUG, ONES : ONES + 1], am_ref.shape)
        mean_e = gram[0:lat, ONES : ONES + 1]
        mean_m = jnp.sum(gram[lat : lat + 3, ONES : ONES + 1], axis=0, keepdims=True)
        c_ref[...] = gram[0:lat] - mean_e * gram[ONES : ONES + 1]
        mrow = jnp.sum(gram[lat : lat + 3], axis=0, keepdims=True)
        cm = jnp.sum(mrow[:, lat : lat + 3], axis=1, keepdims=True) - mean_m * mean_m

        def arrive(i, span):
            copies[i].wait()
            d = nt(x[span], rows) * (1.0 / width)
            mp_ref[span] = jnp.broadcast_to(d[:, ONES : ONES + 1], d.shape)
            sq = jnp.zeros(d.shape, F32)
            for k in range(width // 128):
                p = x[span, k * 128 : (k + 1) * 128].astype(F32)
                sq = sq + p * p
            dt = d.T
            mean_pos = dt[ONES : ONES + 1]
            vp = jnp.sum(sq.T, axis=0, keepdims=True) * (1.0 / width) - mean_pos * mean_pos
            g = dt[0:lat] - mean_e * mean_pos
            gm = jnp.sum(dt[lat : lat + 3], axis=0, keepdims=True) - mean_m * mean_pos
            masked = mask_ref[:, span] == 1
            side_ref[0:lat, span] = jnp.where(masked, 0.0, g)
            side_ref[lat : lat + 8, span] = jnp.concatenate(
                [
                    masked.astype(F32),
                    jnp.where(masked, vp + 2.0 * gm + cm, vp),
                    jnp.zeros((6, g.shape[1]), F32),
                ],
                axis=0,
            )

        project_tile(x, mp_ref, am_ref, w_ref, a_ref, b_ref, r_ref, e_ref, l_ref, arrive)

    @pl.when(pl.program_id(0) > 0)
    def _():
        stay = lambda i, rows: None
        project_tile(x, mp_ref, am_ref, w_ref, a_ref, b_ref, r_ref, e_ref, l_ref, stay)


def value_kernel(pos_ref, aug_ref, mp_ref, am_ref, w_ref, _0, _1, a, b, e, l, r, x, sem):
    proj_kernel(pos_ref, aug_ref, mp_ref, am_ref, w_ref, a, b, r, x, sem, e, l)


def proj_kernel(
    pos_ref, aug_ref, mp_ref, am_ref, w_ref, a_ref, b_ref, r_ref, x, sem, first=None, last=None
):
    tokens = pos_ref.shape[0]
    rest = (x, mp_ref, am_ref, w_ref, a_ref, b_ref, r_ref, first, last)

    @pl.when(pl.program_id(0) == 0)
    def _():
        copies = fetch_rows(pos_ref, x, sem, sem.shape[0])
        for copy in copies:
            copy.start()
        x[pl.ds(tokens, AUG), :] = aug_ref[...]
        project_tile(*rest, lambda i, rows: copies[i].wait())

    @pl.when(pl.program_id(0) > 0)
    def _():
        project_tile(*rest, lambda i, rows: None)


def project(kind, pos, extra, weight, frames, span, into=()):
    tokens, width = pos.shape
    inner = weight.shape[1]
    tile = 256
    steps = inner // tile
    double = kind != "query"
    skip = steps if kind == "value" else 0
    cols = 2 * inner if double else inner
    shapes = (pltpu.HBM((frames, span, inner), BF),) * 2
    specs = (pl.BlockSpec((frames, span, tile), lambda n: (0, 0, n)),) * 2
    if double:
        shapes += (pltpu.HBM((2, span, cols), BF),) * 2
        specs += (pl.BlockSpec((2, span, tile), lambda n: (0, 0, n + skip)),) * 2
    shapes += (jax.ShapeDtypeStruct((64, inner), BF),)
    specs += (pl.BlockSpec((64, tile), lambda n: (0, n)),)
    scratch = [pltpu.VMEM((tokens + AUG, width), BF)]
    pieces = frames
    if kind == "key":
        shapes += (
            jax.ShapeDtypeStruct((EXT - 16, tokens), F32),
            jax.ShapeDtypeStruct((16, 128), F32),
            jax.ShapeDtypeStruct((AUG, width), BF),
            jax.ShapeDtypeStruct((tokens, 128), F32),
            jax.ShapeDtypeStruct((AUG, 128), F32),
        )
        specs += (VM,) * 5
        scratch.append(pltpu.VMEM((128, width), F32))
    scratch.append(pltpu.SemaphoreType.DMA((pieces,)))
    kernel = {"key": front_kernel, "value": value_kernel, "query": proj_kernel}[kind]
    return pl.pallas_call(
        kernel,
        out_shape=shapes,
        grid=(steps,),
        in_specs=[HBM, VM, VM, VM, pl.BlockSpec((width, tile), lambda n: (0, n))]
        + [ANY] * len(into),
        out_specs=specs,
        scratch_shapes=scratch,
        input_output_aliases={5 + i: 2 + i for i in range(len(into))},
        compiler_params=params(24),
        cost_estimate=pl.CostEstimate(
            flops=2 * tokens * width * inner, bytes_accessed=12 * MIB, transcendentals=0
        ),
    )(pos, *extra, weight, *into)


def conv_kernel(sum_ref, gain_ref, bias_ref, x_ref, k_ref, side_ref, o_ref, *, count, per_group, width):
    sums = sum_ref[...]
    channels = sums.shape[1]
    lane = lax.broadcasted_iota(jnp.int32, sums.shape, 1)
    step = 1
    while step < per_group:
        sums = sums + jnp.where(
            (lane & step) == 0, pltpu.roll(sums, channels - step, 1), pltpu.roll(sums, step, 1)
        )
        step *= 2
    average = sums[0:1] * (1.0 / count)
    variance = sums[1:2] * (1.0 / count) - average * average
    inverse = lax.rsqrt(variance + 1e-06)
    scale = inverse * gain_ref[...]
    shift = bias_ref[...] - average * scale
    frames = o_ref.shape[0] - 2
    lat = 16
    cells = x_ref.shape[0] // frames
    o_ref[...] = jnp.zeros_like(o_ref)
    pad = (o_ref.shape[2] - cells) // 2
    w = lax.broadcasted_iota(jnp.int32, (9 * lat, cells), 1) % width
    acc = [None] * (frames + 2)
    for f in range(frames):
        v = x_ref[f * cells : (f + 1) * cells].astype(F32) * scale + shift
        act = (v / (1.0 + jnp.exp(-v))).astype(BF)
        y = nt(k_ref[...], act)
        n = 9 * lat
        y = (
            y[n : 2 * n]
            + jnp.where(w == 0, 0.0, pltpu.roll(y[0:n], 1, 1))
            + jnp.where(w == width - 1, 0.0, pltpu.roll(y[2 * n : 3 * n], cells - 1, 1))
        )
        gap = jnp.zeros((3 * lat, pad), F32)
        m = 3 * lat
        z = [jnp.concatenate([gap, y[b * m : (b + 1) * m], gap], axis=1) for b in range(3)]
        full = z[0].shape[1]
        z = z[1] + pltpu.roll(z[0], width, 1) + pltpu.roll(z[2], full - width, 1)
        for a in range(3):
            part = z[a * lat : (a + 1) * lat]
            i = f - a + 2
            acc[i] = part if acc[i] is None else acc[i] + part
        o_ref[f + 1, lat:EXT, pad : pad + cells] = side_ref[:, f * cells : (f + 1) * cells]
    for i in range(frames + 2):
        o_ref[i, 0:lat] = acc[i]


def columns_of(at, j, span):
    lat = 16
    piece = at[j // 4, :, pl.ds(pl.multiple_of((j % 4) * span, span), span)]
    a = piece.T
    return a.astype(BF), a[:, 2 * lat + 2 : 2 * lat + 3], a[:, 2 * lat + 3 : 2 * lat + 4]


def units(us, eps):
    mean = jnp.full((128, 128), 1.0 / 128, BF)
    squares = [nn((u * u).astype(BF), mean) for u in us]
    eps = jnp.broadcast_to(eps, us[0].shape)
    return [u * lax.rsqrt(s + eps) for u, s in zip(us, squares)]


def cut(h):
    return slice(h * 128, (h + 1) * 128)


def finish_block(j, i, at, rk_ref, rv_ref, raw_k, raw_v, pk, pv):
    heads = pk.shape[2] // 128
    a, rs, eps = columns_of(at, j, pk.shape[1])
    us = [nn(a, rk_ref[:, cut(h)]) + raw_k[:, cut(h)].astype(F32) for h in range(heads)]
    for h, k in enumerate(units(us, eps)):
        pk[i, :, cut(h)] = k.astype(BF)
    rs = jnp.broadcast_to(rs, us[0].shape)
    for h in range(heads):
        v = (nn(a, rv_ref[:, cut(h)]) + raw_v[:, cut(h)].astype(F32)) * rs
        pv[i, :, cut(h)] = v.astype(BF)


def attend_block(q, pk, pv, i, num, den):
    heads = q.shape[1] // 128
    scores = [nt(q[:, cut(h)], pk[i, :, cut(h)]) for h in range(heads)]
    weights = [jnp.exp(s).astype(BF) for s in scores]
    ones = jnp.ones((pv.shape[1], 128), BF)
    sums = [
        nn(w, jnp.concatenate([pv[i, :, cut(h)], ones], axis=1)) for h, w in enumerate(weights)
    ]
    for h in range(heads):
        num[:, cut(h)] += sums[h][:, 0:128]
        den[h] += sums[h][:, 128:]


def near_kernel(
    slot_ref, scale_ref,
    s_ref, up_ref, low_ref, bias_ref, c_ref, rk_ref, rv_ref, rq_ref, qa_ref, qb_ref,
    ka, kb, va, vb,
    q_ref, n_ref, d_ref, at, pk, pv, num, den, ready, *, slots,
):
    block = pl.program_id(0)
    frames = ka.shape[0]
    span = pk.shape[1]
    inner = pk.shape[2]
    heads = inner // 128
    lat = 16

    @pl.when(block == 0)
    def _():
        for j in range(ready.shape[0]):
            ready[j] = 0
        c = c_ref[:, 0:lat]
        ch = c.astype(BF)
        cl = (c - ch.astype(F32)).astype(BF)
        for i in range(frames + 2):
            e = s_ref[i] + jnp.concatenate([up_ref[i], low_ref[i]], axis=1)
            mask = e[2 * lat : 2 * lat + 1]
            latent = (e[0:lat] + bias_ref[...]).astype(BF).astype(F32)
            latent = jnp.where(mask > 0.5, 0.0, latent)
            lb = latent.astype(BF)
            quad = nn(ch, lb) + nn(cl, lb)
            var = e[2 * lat + 1 : 2 * lat + 2] + jnp.sum(
                latent * (2.0 * e[lat : 2 * lat] + quad), axis=0, keepdims=True
            )
            var = jnp.maximum(var, 0.0) + 1e-05
            at[i] = jnp.concatenate(
                [
                    latent,
                    latent,
                    mask,
                    mask,
                    lax.rsqrt(var),
                    1e-06 * var,
                    jnp.zeros((64 - 2 * lat - 4, var.shape[1]), F32),
                ],
                axis=0,
            )

    own = (block // 2 + 1) * 4 + block % 2 + 1
    a, _, eps = columns_of(at, own, span)
    even = block % 2 == 0
    raw = [jnp.where(even, qa_ref[0, :, cut(h)], qb_ref[0, :, cut(h)]) for h in range(heads)]
    us = [nn(a, rq_ref[:, cut(h)]) + r.astype(F32) for h, r in enumerate(raw)]
    for h, q in enumerate(units(us, eps)):
        q_ref[0, :, cut(h)] = (q * scale_ref[h]).astype(BF)
    num[...] = jnp.zeros_like(num)
    den[...] = jnp.zeros_like(den)

    def one(i, _):
        j = slot_ref[block * slots + i]
        f, p = j // 4 - 1, j % 4 - 1

        @pl.when((j >= 0) & (f >= 0) & (f < frames) & (p >= 0) & (p < 2))
        def _():
            n = f * 2 + p

            @pl.when(ready[n] == 0)
            def _():
                ready[n] = 1

                @pl.when(p == 0)
                def _():
                    finish_block(j, n, at, rk_ref, rv_ref, ka.at[f], va.at[f], pk, pv)

                @pl.when(p == 1)
                def _():
                    finish_block(j, n, at, rk_ref, rv_ref, kb.at[f], vb.at[f], pk, pv)

            attend_block(q_ref[0], pk, pv, n, num, den)

        return 0

    lax.fori_loop(0, slots, one, 0)
    n_ref[0] = num[...]
    d_ref[0] = jnp.concatenate([den[h, :, 0:1] for h in range(heads)], axis=1)


def far_kernel(
    slot_ref, true_ref,
    q_ref, n_ref, d_ref, at, rk_ref, rv_ref, ku, kd, vu, vd, kf, kz, kg, kh, kc,
    o_ref, raw, pk, pv, num, den, need, sem, *, slots,
):
    block = pl.program_id(0)
    frames = ku.shape[0]
    inner = pk.shape[2]
    heads = inner // 128
    total = pk.shape[0]

    def local(j):
        return 0 <= j // 4 - 1 < frames and 1 <= j % 4 <= 2

    def source(j):
        f, q = j // 4 - 1, j % 4
        late = f >= 0
        if q == 3:
            return kc.at[int(late)]
        if q == 0:
            return (kh if late else kg).at[0]
        return (kz if late else kf).at[q - 1]

    @pl.when(block == 0)
    def _():
        for j in range(total):
            need[j] = 0

        def mark(i, _):
            j = slot_ref[i]

            @pl.when(j >= 0)
            def _():
                need[j] = 1

            return 0

        lax.fori_loop(0, slot_ref.shape[0], mark, 0)
        for j in range(total):
            if local(j):
                continue

            @pl.when(need[j] == 1)
            def _(j=j):
                f = j // 4 - 1
                if 0 <= f < frames:
                    k, v = (kd, vd) if j % 4 else (ku, vu)
                    pltpu.make_async_copy(k.at[f], raw.at[j, :, 0:inner], sem.at[j]).start()
                    pltpu.make_async_copy(v.at[f], raw.at[j, :, inner:], sem.at[j]).start()
                else:
                    pltpu.make_async_copy(source(j), raw.at[j], sem.at[j]).start()

    num[...] = n_ref[0]
    den[...] = jnp.zeros_like(den)

    def one(i, _):
        j = slot_ref[block * slots + i]
        f, p = j // 4 - 1, j % 4 - 1
        inside = (f >= 0) & (f < frames) & (p >= 0) & (p < 2)

        @pl.when((j >= 0) & ~inside)
        def _():
            @pl.when(need[j] == 1)
            def _():
                need[j] = 2
                pltpu.make_async_copy(kf.at[0], raw.at[j], sem.at[j]).wait()
                k, v = raw.at[j, :, 0:inner], raw.at[j, :, inner:]
                finish_block(true_ref[j], j, at, rk_ref, rv_ref, k, v, pk, pv)

            attend_block(q_ref[0], pk, pv, j, num, den)

        return 0

    lax.fori_loop(0, slots, one, 0)
    whole = [den[h] + d_ref[0, :, h : h + 1] for h in range(heads)]
    for h in range(heads):
        o_ref[0, :, cut(h)] = (num[:, cut(h)] / whole[h]).astype(BF)


def shift(values, axis, by):
    edges = range(lax.axis_size(axis) - 1)
    pairs = [(i, i + 1) if by > 0 else (i + 1, i) for i in edges]
    return lax.ppermute(values, axis, pairs)


def swap(values, axis, bit):
    count = lax.axis_size(axis)
    return lax.ppermute(values, axis, [(i, i ^ bit) for i in range(count)])


def round_bits(row_count, time_count):
    doubling = lambda bit, count: [bit << i for i in range(count) if bit << i < count]
    apart = [("row", bit) for bit in doubling(2, row_count)]
    rest = [("row", 1)] + [("tm", bit) for bit in doubling(1, time_count)]
    return apart, rest


def per_device(
    features,
    norm_gain,
    norm_bias,
    latent_kernel,
    latent_bias,
    token_mask,
    embed_weight,
    mask_token,
    pos_embed,
    query_weight,
    key_weight,
    value_weight,
    logit_scale,
    pattern,
):
    frames, slab_rows, row_width, channels = features.shape
    per_group = channels // GROUPS
    time_count = lax.axis_size("tm")
    row_count = lax.axis_size("row")
    time_index = lax.axis_index("tm")
    row_index = lax.axis_index("row")
    tokens = frames * slab_rows * row_width
    latents, width = embed_weight.shape
    heads = logit_scale.shape[0]
    inner = query_weight.shape[1]
    row_pairs = slab_rows // 2
    span = 2 * row_width
    blocks = frames * row_pairs
    slots = pattern.shape[-1]
    cell_count = frames * time_count * slab_rows * row_count * row_width * per_group

    flat = features.reshape(tokens, channels)
    sums = pl.pallas_call(
        stats_kernel,
        out_shape=jax.ShapeDtypeStruct((2, channels), F32),
        grid=(4,),
        in_specs=[pl.BlockSpec((tokens // 4, channels), lambda i: (i, 0))],
        out_specs=pl.BlockSpec((2, channels), lambda i: (0, 0)),
        compiler_params=params(4),
    )(flat)
    far_rounds, close_rounds = round_bits(row_count, time_count)
    rounds = far_rounds + close_rounds
    apart = len(far_rounds)

    def after(value, *others):
        return lax.optimization_barrier((value, *others))[0]

    def advance(value, step):
        axis, bit = rounds[step]
        return value + swap(value, axis, bit)

    hbm = lambda x: pltpu.with_memory_space_constraint(x, pltpu.HBM)
    pos = hbm(pos_embed.reshape(tokens, width))
    steps = [sums, advance(sums, 0)]
    front = project(
        "key", pos,
        (after(embed_weight, sums), mask_token.reshape(1, -1), token_mask.reshape(1, -1)),
        hbm(key_weight), frames, span,
    )
    ka, kb = front[:2]
    rk, side, gram = front[4:7]
    extra = front[7:]
    steps[1] = after(steps[1], gram)
    for step in range(1, len(rounds)):
        steps.append(advance(steps[-1], step))
    sums = steps[-1]
    up_k = shift(after(kb, steps[apart]), "row", 1)
    down_k = shift(after(ka, steps[apart]), "row", -1)
    va, vb, edge, last, rv = project(
        "value", pos, (after(extra[0], steps[apart + 1]), *extra[1:]), hbm(value_weight), frames,
        span, front[2:4],
    )
    qa, qb, rq = project(
        "query", pos, (after(extra[0], va), *extra[1:]), hbm(query_weight), frames, span
    )

    taps = latent_kernel.transpose(3, 2, 1, 0, 4).reshape(27 * latents, channels)
    reach = (slab_rows + 4) * row_width
    local = pl.pallas_call(
        functools.partial(conv_kernel, count=cell_count, per_group=per_group, width=row_width),
        out_shape=jax.ShapeDtypeStruct((frames + 2, EXT, reach), F32),
        in_specs=[VM] * 6,
        out_specs=VM,
        compiler_params=params(14),
    )(sums, norm_gain.reshape(1, -1), norm_bias.reshape(1, -1), flat, taps, side)
    fore = shift(local[frames:], "tm", 1)
    aft = shift(local[:2], "tm", -1)
    blank = jnp.zeros((frames - 2, *local.shape[1:]), F32)
    tall = local + jnp.concatenate([fore, blank, aft], axis=0)
    half = reach // 2
    upper = shift(tall[:, :, half:], "row", 1)
    lower = shift(tall[:, :, :half], "row", -1)
    fwd = shift(last, "tm", 1)
    back = shift(edge, "tm", -1)
    up_v = shift(vb, "row", 1)
    down_v = shift(va, "row", -1)
    even = row_index % 2 == 0

    pair_total = row_pairs * row_count
    listed = pattern.reshape(blocks, slots)
    clamped = jnp.maximum(listed, 0)
    key_frame = clamped // pair_total - time_index * frames + 1
    key_pair = clamped % pair_total - row_index * row_pairs + 1
    across = (key_frame == 0) | (key_frame == frames + 1)
    edge = (key_pair == 0) | (key_pair == 3)
    place = jnp.where(across & edge & ~even, 3 - key_pair, key_pair)
    slot = jnp.where(listed >= 0, key_frame * 4 + place, -1).reshape(-1)
    ids = jnp.arange((frames + 2) * 4)
    id_frame, id_pair = ids // 4, ids % 4
    flip = ((id_frame == 0) | (id_frame == frames + 1)) & ((id_pair == 0) | (id_pair == 3)) & ~even
    true_id = jnp.where(flip, id_frame * 4 + 3 - id_pair, ids)
    total = (frames + 2) * 4

    each = lambda b, *_: (b, 0, 0)
    half_block = pl.BlockSpec((1, span, inner), lambda b, *_: (b // 2, 0, 0))
    whole_block = pl.BlockSpec((1, span, inner), each)
    den_block = pl.BlockSpec((1, span, heads), each)
    near = pl.pallas_call(
        functools.partial(near_kernel, slots=slots),
        out_shape=(
            jax.ShapeDtypeStruct((blocks, span, inner), BF),
            jax.ShapeDtypeStruct((blocks, span, inner), F32),
            jax.ShapeDtypeStruct((blocks, span, heads), F32),
            jax.ShapeDtypeStruct((frames + 2, 64, reach), F32),
        ),
        grid_spec=pltpu.PrefetchScalarGridSpec(
            num_scalar_prefetch=2,
            grid=(blocks,),
            in_specs=[VM] * 8 + [half_block] * 2 + [VM] * 4,
            out_specs=(whole_block, whole_block, den_block, VM),
            scratch_shapes=[
                pltpu.VMEM((blocks, span, inner), BF),
                pltpu.VMEM((blocks, span, inner), BF),
                pltpu.VMEM((span, inner), F32),
                pltpu.VMEM((heads, span, 128), F32),
                pltpu.SMEM((blocks,), jnp.int32),
            ],
        ),
        compiler_params=params(26),
        cost_estimate=pl.CostEstimate(flops=16 * 10**9, bytes_accessed=16 * MIB, transcendentals=0),
    )
    query, num, den, cols = near(
        slot, logit_scale / (inner // heads),
        tall, upper, lower, latent_bias.reshape(-1, 1), gram, rk, rv, rq, qa, qb,
        ka, kb, va, vb,
    )

    def outer(i):
        pick = lambda u, d: jnp.where(even, u[i], d[i])
        return jnp.concatenate([pick(up_k, down_k), pick(up_v, down_v)], axis=-1)[None]

    outer_fwd = shift(outer(-1), "tm", 1)
    outer_back = shift(outer(0), "tm", -1)
    corner = jnp.stack([jnp.where(even, fwd[1], fwd[0]), jnp.where(even, back[1], back[0])])
    corner = swap(corner, "row", 1)

    out = pl.pallas_call(
        functools.partial(far_kernel, slots=slots),
        out_shape=jax.ShapeDtypeStruct((blocks, span, inner), BF),
        grid_spec=pltpu.PrefetchScalarGridSpec(
            num_scalar_prefetch=2,
            grid=(blocks,),
            in_specs=[whole_block, whole_block, den_block, VM, VM, VM] + [ANY] * 9,
            out_specs=whole_block,
            scratch_shapes=[
                pltpu.VMEM((total, span, 2 * inner), BF),
                pltpu.VMEM((total, span, inner), BF),
                pltpu.VMEM((total, span, inner), BF),
                pltpu.VMEM((span, inner), F32),
                pltpu.VMEM((heads, span, 128), F32),
                pltpu.SMEM((total,), jnp.int32),
                pltpu.SemaphoreType.DMA((total,)),
            ],
        ),
        compiler_params=params(38),
    )(
        slot, true_id, query, num, den, cols, rk, rv,
        up_k, down_k, up_v, down_v, fwd, back, outer_fwd, outer_back, corner,
    )
    return out.reshape(frames, slab_rows, row_width, inner)


def solution(mesh):
    in_specs = (
        P("tm", "row", None, None),
        P(),
        P(),
        P(),
        P(),
        P("tm", "row", None),
        P(),
        P(),
        P("tm", "row", None, None),
        P(),
        P(),
        P(),
        P(),
        P("tm", "row", None),
    )
    out_specs = P("tm", "row", None, None)

    return jax.shard_map(
        per_device, mesh=mesh, in_specs=in_specs, out_specs=out_specs, check_vma=False
    )
```

```python
import functools

import jax
import jax.numpy as jnp
from jax import lax
from jax.experimental import pallas as pl
from jax.experimental.pallas import tpu as pltpu
from jax.sharding import PartitionSpec as P


GROUPS = 32
BF = jnp.bfloat16
F32 = jnp.float32
VM = pl.BlockSpec(memory_space=pltpu.VMEM)
SM = pl.BlockSpec(memory_space=pltpu.SMEM)
ANY = pl.BlockSpec(memory_space=pl.ANY)
HBM = pl.BlockSpec(memory_space=pltpu.HBM)
AUG = 32
ONES = 19
EXT = 40
MIB = 1 << 20


def params(mib):
    return pltpu.CompilerParams(vmem_limit_bytes=mib * MIB)


def nt(a, b):
    return lax.dot_general(a, b, (((1,), (1,)), ((), ())), preferred_element_type=F32)


def nn(a, b):
    return lax.dot_general(a, b, (((1,), (0,)), ((), ())), preferred_element_type=F32)


def stats_kernel(x_ref, o_ref):
    @pl.when(pl.program_id(0) == 0)
    def _():
        o_ref[...] = jnp.zeros_like(o_ref)

    x = x_ref[...].astype(F32)
    o_ref[0:1] += jnp.sum(x, axis=0, keepdims=True)
    o_ref[1:2] += jnp.sum(x * x, axis=0, keepdims=True)


def fetch_rows(pos_ref, x, sem, pieces):
    rows = pos_ref.shape[0] // pieces
    return [
        pltpu.make_async_copy(
            pos_ref.at[pl.ds(i * rows, rows)], x.at[pl.ds(i * rows, rows)], sem.at[i]
        )
        for i in range(pieces)
    ]


def project_tile(x, mp, am, w_ref, a_ref, b_ref, r_ref, first, last, arrive):
    lat = 16
    frames, span, tile = a_ref.shape
    tokens = x.shape[0] - AUG
    aw = nn(x[pl.ds(tokens, AUG)], w_ref[...])
    colsum = aw[ONES : ONES + 1]
    ew = aw[0:lat] - am[0:lat, 0:1] * colsum
    mw = jnp.sum(aw[lat : lat + 3], axis=0, keepdims=True)
    mean_m = jnp.sum(am[lat : lat + 3, 0:1], axis=0, keepdims=True)
    mw = mw - mean_m * colsum
    ewh = ew.astype(BF).astype(F32)
    mwh = mw.astype(BF).astype(F32)
    r_ref[0:lat] = ewh.astype(BF)
    r_ref[lat : 2 * lat] = (ew - ewh).astype(BF)
    r_ref[2 * lat : 4 * lat] = jnp.concatenate(
        [mwh, mw - mwh, jnp.zeros((2 * lat - 2, mw.shape[1]), F32)], axis=0
    ).astype(BF)
    for f in range(frames):
        rows = slice(2 * f * span, (2 * f + 2) * span)
        arrive(f, rows)
        acc = nn(x[rows], w_ref[...])
        for k in range(tile // 128):
            part = (acc[:, cut(k)] - mp[rows] * colsum[:, cut(k)]).astype(BF)
            a_ref[f, :, cut(k)] = part[0:span]
            b_ref[f, :, cut(k)] = part[span:]
            edge = {0: first, frames - 1: last}.get(f)
            if edge is not None:
                edge[0, :, cut(k)] = part[0:span]
                edge[1, :, cut(k)] = part[span:]


def front_kernel(pos_ref, embed_ref, mtok_ref, mask_ref, w_ref, a_ref, b_ref, e_ref, l_ref, r_ref,
                 side_ref, c_ref, aug_ref, mp_ref, am_ref, x, aug, sem):
    tokens = pos_ref.shape[0]
    lat, width = embed_ref.shape
    pieces = sem.shape[0]

    @pl.when(pl.program_id(0) == 0)
    def _():
        copies = fetch_rows(pos_ref, x, sem, pieces)
        for copy in copies:
            copy.start()
        aug[...] = jnp.zeros_like(aug)
        aug[0:lat] = embed_ref[...].astype(F32)
        m = mtok_ref[...]
        hi = m.astype(BF).astype(F32)
        mid = (m - hi).astype(BF).astype(F32)
        low = (m - hi - mid).astype(BF).astype(F32)
        aug[lat : lat + 1] = hi
        aug[lat + 1 : lat + 2] = mid
        aug[lat + 2 : lat + 3] = low
        aug[ONES : ONES + 1] = jnp.ones_like(hi)
        rows = aug[...].astype(BF)
        x[pl.ds(tokens, AUG), :] = rows[0:AUG]
        aug_ref[...] = rows[0:AUG]
        gram = nt(rows, rows) * (1.0 / width)
        am_ref[...] = jnp.broadcast_to(gram[0:AUG, ONES : ONES + 1], am_ref.shape)
        mean_e = gram[0:lat, ONES : ONES + 1]
        mean_m = jnp.sum(gram[lat : lat + 3, ONES : ONES + 1], axis=0, keepdims=True)
        c_ref[...] = gram[0:lat] - mean_e * gram[ONES : ONES + 1]
        mrow = jnp.sum(gram[lat : lat + 3], axis=0, keepdims=True)
        cm = jnp.sum(mrow[:, lat : lat + 3], axis=1, keepdims=True) - mean_m * mean_m

        def arrive(i, span):
            copies[i].wait()
            d = nt(x[span], rows) * (1.0 / width)
            mp_ref[span] = jnp.broadcast_to(d[:, ONES : ONES + 1], d.shape)
            sq = jnp.zeros(d.shape, F32)
            for k in range(width // 128):
                p = x[span, k * 128 : (k + 1) * 128].astype(F32)
                sq = sq + p * p
            dt = d.T
            mean_pos = dt[ONES : ONES + 1]
            vp = jnp.sum(sq.T, axis=0, keepdims=True) * (1.0 / width) - mean_pos * mean_pos
            g = dt[0:lat] - mean_e * mean_pos
            gm = jnp.sum(dt[lat : lat + 3], axis=0, keepdims=True) - mean_m * mean_pos
            masked = mask_ref[:, span] == 1
            side_ref[0:lat, span] = jnp.where(masked, 0.0, g)
            side_ref[lat : lat + 8, span] = jnp.concatenate(
                [
                    masked.astype(F32),
                    jnp.where(masked, vp + 2.0 * gm + cm, vp),
                    jnp.zeros((6, g.shape[1]), F32),
                ],
                axis=0,
            )

        project_tile(x, mp_ref, am_ref, w_ref, a_ref, b_ref, r_ref, e_ref, l_ref, arrive)

    @pl.when(pl.program_id(0) > 0)
    def _():
        stay = lambda i, rows: None
        project_tile(x, mp_ref, am_ref, w_ref, a_ref, b_ref, r_ref, e_ref, l_ref, stay)


def value_query_kernel(pos_ref, aug_ref, mp_ref, am_ref, w_ref, q_ref, _0, _1,
                       a, b, e, l, r, qa, qb, qr, x, sem):
    tokens = pos_ref.shape[0]
    step = pl.program_id(0)
    half = pl.num_programs(0) // 2
    rest = (x, mp_ref, am_ref, w_ref, a, b, r, e, l)

    @pl.when(step == 0)
    def _():
        copies = fetch_rows(pos_ref, x, sem, sem.shape[0])
        for copy in copies:
            copy.start()
        x[pl.ds(tokens, AUG), :] = aug_ref[...]
        project_tile(*rest, lambda i, rows: copies[i].wait())

    @pl.when((step > 0) & (step < half))
    def _():
        project_tile(*rest, lambda i, rows: None)

    @pl.when(step >= half)
    def _():
        project_tile(x, mp_ref, am_ref, q_ref, qa, qb, qr, None, None, lambda i, rows: None)


def project(pos, extra, weights, frames, span, into=()):
    tokens, width = pos.shape
    inner = weights[0].shape[1]
    tile = 256
    steps = inner // tile
    keys = len(weights) == 1
    skip = 0 if keys else steps
    whole = lambda array: pl.BlockSpec(array.shape, lambda n: (0, 0))
    early = lambda n: jnp.minimum(n, steps - 1)
    late = lambda n: jnp.maximum(n - steps, 0)

    def outputs(pick):
        shape = pltpu.HBM((frames, span, inner), BF)
        spec = pl.BlockSpec((frames, span, tile), lambda n: (0, 0, pick(n)))
        rows = jax.ShapeDtypeStruct((64, inner), BF)
        return (shape, shape, rows), (spec, spec, pl.BlockSpec((64, tile), lambda n: (0, pick(n))))

    (shape, _, row_shape), (spec, _, row_spec) = outputs(early)
    edge = pl.BlockSpec((2, span, tile), lambda n: (0, 0, early(n) + skip))
    shapes = (shape, shape) + (pltpu.HBM((2, span, 2 * inner), BF),) * 2 + (row_shape,)
    specs = (spec, spec, edge, edge, row_spec)
    tiles = [pl.BlockSpec((width, tile), lambda n: (0, early(n)))]
    scratch = [pltpu.VMEM((tokens + AUG, width), BF)]
    if keys:
        shapes += (
            jax.ShapeDtypeStruct((EXT - 16, tokens), F32),
            jax.ShapeDtypeStruct((16, 128), F32),
            pltpu.HBM((AUG, width), BF),
            pltpu.HBM((tokens, 128), F32),
            pltpu.HBM((AUG, 128), F32),
        )
        specs += (VM, VM) + tuple(whole(shape) for shape in shapes[-3:])
        scratch.append(pltpu.VMEM((128, width), F32))
    else:
        more = outputs(late)
        shapes += more[0]
        specs += more[1]
        tiles.append(pl.BlockSpec((width, tile), lambda n: (0, late(n))))
    scratch.append(pltpu.SemaphoreType.DMA((frames,)))
    return pl.pallas_call(
        front_kernel if keys else value_query_kernel,
        out_shape=shapes,
        grid=(steps * len(weights),),
        in_specs=[HBM] + [whole(array) for array in extra] + tiles + [ANY] * len(into),
        out_specs=specs,
        scratch_shapes=scratch,
        input_output_aliases={4 + len(weights) + i: 2 + i for i in range(len(into))},
        compiler_params=params(24),
        cost_estimate=pl.CostEstimate(
            flops=2 * tokens * width * inner * len(weights), bytes_accessed=12 * MIB,
            transcendentals=0,
        ),
    )(pos, *extra, *weights, *into)


def conv_kernel(sum_ref, gain_ref, bias_ref, x_ref, k_ref, side_ref, o_ref, *, count, per_group, width):
    sums = sum_ref[...]
    channels = sums.shape[1]
    lane = lax.broadcasted_iota(jnp.int32, sums.shape, 1)
    step = 1
    while step < per_group:
        sums = sums + jnp.where(
            (lane & step) == 0, pltpu.roll(sums, channels - step, 1), pltpu.roll(sums, step, 1)
        )
        step *= 2
    average = sums[0:1] * (1.0 / count)
    variance = sums[1:2] * (1.0 / count) - average * average
    inverse = lax.rsqrt(variance + 1e-06)
    scale = inverse * gain_ref[...]
    shift = bias_ref[...] - average * scale
    frames = o_ref.shape[0] - 2
    lat = 16
    cells = x_ref.shape[0] // frames
    o_ref[...] = jnp.zeros_like(o_ref)
    pad = (o_ref.shape[2] - cells) // 2
    w = lax.broadcasted_iota(jnp.int32, (9 * lat, cells), 1) % width
    acc = [None] * (frames + 2)
    for f in range(frames):
        v = x_ref[f * cells : (f + 1) * cells].astype(F32) * scale + shift
        act = (v / (1.0 + jnp.exp(-v))).astype(BF)
        y = nt(k_ref[...], act)
        n = 9 * lat
        y = (
            y[n : 2 * n]
            + jnp.where(w == 0, 0.0, pltpu.roll(y[0:n], 1, 1))
            + jnp.where(w == width - 1, 0.0, pltpu.roll(y[2 * n : 3 * n], cells - 1, 1))
        )
        gap = jnp.zeros((3 * lat, pad), F32)
        m = 3 * lat
        z = [jnp.concatenate([gap, y[b * m : (b + 1) * m], gap], axis=1) for b in range(3)]
        full = z[0].shape[1]
        z = z[1] + pltpu.roll(z[0], width, 1) + pltpu.roll(z[2], full - width, 1)
        for a in range(3):
            part = z[a * lat : (a + 1) * lat]
            i = f - a + 2
            acc[i] = part if acc[i] is None else acc[i] + part
        o_ref[f + 1, lat:EXT, pad : pad + cells] = side_ref[:, f * cells : (f + 1) * cells]
    for i in range(frames + 2):
        o_ref[i, 0:lat] = acc[i]


def columns_of(at, j, span):
    lat = 16
    piece = at[j // 4, :, pl.ds(pl.multiple_of((j % 4) * span, span), span)]
    a = piece.T
    return a.astype(BF), a[:, 2 * lat + 2 : 2 * lat + 3], a[:, 2 * lat + 3 : 2 * lat + 4]


def units(us, eps):
    mean = jnp.full((128, 128), 1.0 / 128, BF)
    squares = [nn((u * u).astype(BF), mean) for u in us]
    eps = jnp.broadcast_to(eps, us[0].shape)
    return [u * lax.rsqrt(s + eps) for u, s in zip(us, squares)]


def cut(h):
    return slice(h * 128, (h + 1) * 128)


def finish_block(j, i, at, rk_ref, rv_ref, raw_k, raw_v, pk, pv):
    heads = pk.shape[2] // 128
    a, rs, eps = columns_of(at, j, pk.shape[1])
    us = [nn(a, rk_ref[:, cut(h)]) + raw_k[:, cut(h)].astype(F32) for h in range(heads)]
    for h, k in enumerate(units(us, eps)):
        pk[i, :, cut(h)] = k.astype(BF)
    rs = jnp.broadcast_to(rs, us[0].shape)
    for h in range(heads):
        v = (nn(a, rv_ref[:, cut(h)]) + raw_v[:, cut(h)].astype(F32)) * rs
        pv[i, :, cut(h)] = v.astype(BF)


def attend_block(q, pk, pv, i, num, den, start=False):
    heads = q.shape[1] // 128
    scores = [nt(q[:, cut(h)], pk[i, :, cut(h)]) for h in range(heads)]
    weights = [jnp.exp(s).astype(BF) for s in scores]
    ones = jnp.ones((pv.shape[1], 128), BF)
    sums = [
        nn(w, jnp.concatenate([pv[i, :, cut(h)], ones], axis=1)) for h, w in enumerate(weights)
    ]
    for h in range(heads):
        if start:
            num[:, cut(h)] = sums[h][:, 0:128]
            den[h] = sums[h][:, 128:]
        else:
            num[:, cut(h)] += sums[h][:, 0:128]
            den[h] += sums[h][:, 128:]


def near_kernel(
    slot_ref, scale_ref,
    s_ref, up_ref, low_ref, bias_ref, c_ref, rk_ref, rv_ref, rq_ref, qa_ref, qb_ref,
    ka, kb, va, vb,
    q_ref, n_ref, d_ref, at, pk, pv, den, ready, *, slots,
):
    block = pl.program_id(0)
    frames = ka.shape[0]
    span = pk.shape[1]
    inner = pk.shape[2]
    heads = inner // 128
    lat = 16

    @pl.when(block == 0)
    def _():
        for j in range(ready.shape[0]):
            ready[j] = 0
        c = c_ref[:, 0:lat]
        ch = c.astype(BF)
        cl = (c - ch.astype(F32)).astype(BF)
        for i in range(frames + 2):
            e = s_ref[i] + jnp.concatenate([up_ref[i], low_ref[i]], axis=1)
            mask = e[2 * lat : 2 * lat + 1]
            latent = (e[0:lat] + bias_ref[...]).astype(BF).astype(F32)
            latent = jnp.where(mask > 0.5, 0.0, latent)
            lb = latent.astype(BF)
            quad = nn(ch, lb) + nn(cl, lb)
            var = e[2 * lat + 1 : 2 * lat + 2] + jnp.sum(
                latent * (2.0 * e[lat : 2 * lat] + quad), axis=0, keepdims=True
            )
            var = jnp.maximum(var, 0.0) + 1e-05
            at[i] = jnp.concatenate(
                [
                    latent,
                    latent,
                    mask,
                    mask,
                    lax.rsqrt(var),
                    1e-06 * var,
                    jnp.zeros((64 - 2 * lat - 4, var.shape[1]), F32),
                ],
                axis=0,
            )

    own = (block // 2 + 1) * 4 + block % 2 + 1
    a, _, eps = columns_of(at, own, span)
    even = block % 2 == 0
    raw = [jnp.where(even, qa_ref[0, :, cut(h)], qb_ref[0, :, cut(h)]) for h in range(heads)]
    us = [nn(a, rq_ref[:, cut(h)]) + r.astype(F32) for h, r in enumerate(raw)]
    for h, q in enumerate(units(us, eps)):
        q_ref[0, :, cut(h)] = (q * scale_ref[h]).astype(BF)
    num = n_ref.at[0]

    def prepare(j, f, p):
        n = f * 2 + p

        @pl.when((ready[n] == 0) & (p == 0))
        def _():
            finish_block(j, n, at, rk_ref, rv_ref, ka.at[f], va.at[f], pk, pv)

        @pl.when((ready[n] == 0) & (p == 1))
        def _():
            finish_block(j, n, at, rk_ref, rv_ref, kb.at[f], vb.at[f], pk, pv)

        ready[n] = 1
        return n

    n = prepare(own, block // 2, block % 2)
    attend_block(q_ref[0], pk, pv, n, num, den, True)

    def one(i, _):
        j = slot_ref[block * slots + i]
        f, p = j // 4 - 1, j % 4 - 1

        @pl.when((j >= 0) & (f >= 0) & (f < frames) & (p >= 0) & (p < 2))
        def _():
            n = prepare(j, f, p)
            attend_block(q_ref[0], pk, pv, n, num, den)

        return 0

    lax.fori_loop(1, slots, one, 0)
    d_ref[0] = jnp.concatenate([den[h, :, 0:1] for h in range(heads)], axis=1)


def far_kernel(
    slot_ref, true_ref,
    q_ref, n_ref, d_ref, at, rk_ref, rv_ref, ku, kd, vu, vd, kf, kz, kg, kh, kc,
    o_ref, raw, pk, pv, num, den, need, sem, *, slots,
):
    block = pl.program_id(0)
    frames = ku.shape[0]
    inner = pk.shape[2]
    heads = inner // 128
    total = pk.shape[0]

    def local(j):
        return 0 <= j // 4 - 1 < frames and 1 <= j % 4 <= 2

    def source(j):
        f, q = j // 4 - 1, j % 4
        late = f >= 0
        if q == 3:
            return kc.at[int(late)]
        if q == 0:
            return (kh if late else kg).at[0]
        return (kz if late else kf).at[q - 1]

    @pl.when(block == 0)
    def _():
        for j in range(total):
            need[j] = 0

        def mark(i, _):
            j = slot_ref[i]

            @pl.when(j >= 0)
            def _():
                need[j] = 1

            return 0

        lax.fori_loop(0, slot_ref.shape[0], mark, 0)
        for j in range(total):
            if local(j):
                continue

            @pl.when(need[j] == 1)
            def _(j=j):
                f = j // 4 - 1
                if 0 <= f < frames:
                    k, v = (kd, vd) if j % 4 else (ku, vu)
                    pltpu.make_async_copy(k.at[f], raw.at[j, :, 0:inner], sem.at[j]).start()
                    pltpu.make_async_copy(v.at[f], raw.at[j, :, inner:], sem.at[j]).start()
                else:
                    pltpu.make_async_copy(source(j), raw.at[j], sem.at[j]).start()

    num[...] = n_ref[0]
    den[...] = jnp.zeros_like(den)

    def one(i, _):
        j = slot_ref[block * slots + i]
        f, p = j // 4 - 1, j % 4 - 1
        inside = (f >= 0) & (f < frames) & (p >= 0) & (p < 2)

        @pl.when((j >= 0) & ~inside)
        def _():
            @pl.when(need[j] == 1)
            def _():
                need[j] = 2
                pltpu.make_async_copy(kf.at[0], raw.at[j], sem.at[j]).wait()
                k, v = raw.at[j, :, 0:inner], raw.at[j, :, inner:]
                finish_block(true_ref[j], j, at, rk_ref, rv_ref, k, v, pk, pv)

            attend_block(q_ref[0], pk, pv, j, num, den)

        return 0

    lax.fori_loop(1, slots, one, 0)
    whole = [den[h] + d_ref[0, :, h : h + 1] for h in range(heads)]
    for h in range(heads):
        o_ref[0, :, cut(h)] = (num[:, cut(h)] / whole[h]).astype(BF)


def shift(values, axis, by):
    edges = range(lax.axis_size(axis) - 1)
    pairs = [(i, i + 1) if by > 0 else (i + 1, i) for i in edges]
    return lax.ppermute(values, axis, pairs)


def swap(values, axis, bit):
    count = lax.axis_size(axis)
    return lax.ppermute(values, axis, [(i, i ^ bit) for i in range(count)])


def round_bits(row_count, time_count):
    doubling = lambda bit, count: [bit << i for i in range(count) if bit << i < count]
    apart = [("row", bit) for bit in doubling(2, row_count)]
    rest = [("row", 1)] + [("tm", bit) for bit in doubling(1, time_count)]
    return apart, rest


def per_device(
    features,
    norm_gain,
    norm_bias,
    latent_kernel,
    latent_bias,
    token_mask,
    embed_weight,
    mask_token,
    pos_embed,
    query_weight,
    key_weight,
    value_weight,
    logit_scale,
    pattern,
):
    frames, slab_rows, row_width, channels = features.shape
    per_group = channels // GROUPS
    time_count = lax.axis_size("tm")
    row_count = lax.axis_size("row")
    time_index = lax.axis_index("tm")
    row_index = lax.axis_index("row")
    tokens = frames * slab_rows * row_width
    latents, width = embed_weight.shape
    heads = logit_scale.shape[0]
    inner = query_weight.shape[1]
    row_pairs = slab_rows // 2
    span = 2 * row_width
    blocks = frames * row_pairs
    slots = pattern.shape[-1]
    cell_count = frames * time_count * slab_rows * row_count * row_width * per_group

    flat = features.reshape(tokens, channels)
    sums = pl.pallas_call(
        stats_kernel,
        out_shape=jax.ShapeDtypeStruct((2, channels), F32),
        grid=(4,),
        in_specs=[pl.BlockSpec((tokens // 4, channels), lambda i: (i, 0))],
        out_specs=pl.BlockSpec((2, channels), lambda i: (0, 0)),
        compiler_params=params(4),
    )(pltpu.with_memory_space_constraint(flat, pltpu.HBM))
    far_rounds, close_rounds = round_bits(row_count, time_count)
    rounds = far_rounds + close_rounds
    apart = len(far_rounds)

    def after(value, *others):
        return lax.optimization_barrier((value, *others))[0]

    def advance(value, step):
        axis, bit = rounds[step]
        return value + swap(value, axis, bit)

    hbm = lambda x: pltpu.with_memory_space_constraint(x, pltpu.HBM)
    pos = hbm(pos_embed.reshape(tokens, width))
    steps = [sums, advance(sums, 0)]
    front = project(
        pos,
        (
            hbm(after(embed_weight, sums)), hbm(mask_token.reshape(1, -1)),
            token_mask.reshape(1, -1),
        ),
        (hbm(key_weight),), frames, span,
    )
    ka, kb = front[:2]
    rk, side, gram = front[4:7]
    extra = [hbm(array) for array in front[7:]]
    taps = latent_kernel.transpose(3, 2, 1, 0, 4).reshape(27 * latents, channels)
    steps[1] = after(steps[1], gram, taps)
    for step in range(1, len(rounds)):
        steps.append(advance(steps[-1], step))
    sums = steps[-1]
    up_k = shift(after(kb, steps[apart]), "row", 1)
    down_k = shift(after(ka, steps[apart]), "row", -1)
    va, vb, edge, last, rv, qa, qb, rq = project(
        pos, (hbm(after(extra[0], steps[apart + 1])), *extra[1:]),
        (hbm(value_weight), hbm(query_weight)), frames, span, front[2:4],
    )

    reach = (slab_rows + 4) * row_width
    local = pl.pallas_call(
        functools.partial(conv_kernel, count=cell_count, per_group=per_group, width=row_width),
        out_shape=jax.ShapeDtypeStruct((frames + 2, EXT, reach), F32),
        in_specs=[VM] * 6,
        out_specs=VM,
        compiler_params=params(14),
    )(sums, norm_gain.reshape(1, -1), norm_bias.reshape(1, -1), flat, taps, side)
    fore = shift(local[frames:], "tm", 1)
    aft = shift(local[:2], "tm", -1)
    blank = jnp.zeros((frames - 2, *local.shape[1:]), F32)
    tall = local + jnp.concatenate([fore, blank, aft], axis=0)
    half = reach // 2
    upper = shift(tall[:, :, half:], "row", 1)
    lower = shift(tall[:, :, :half], "row", -1)
    fwd = shift(last, "tm", 1)
    back = shift(edge, "tm", -1)
    up_v = shift(vb, "row", 1)
    down_v = shift(va, "row", -1)
    even = row_index % 2 == 0

    pair_total = row_pairs * row_count
    listed = pattern.reshape(blocks, slots)
    clamped = jnp.maximum(listed, 0)
    key_frame = clamped // pair_total - time_index * frames + 1
    key_pair = clamped % pair_total - row_index * row_pairs + 1
    across = (key_frame == 0) | (key_frame == frames + 1)
    edge = (key_pair == 0) | (key_pair == 3)
    place = jnp.where(across & edge & ~even, 3 - key_pair, key_pair)
    slot = jnp.where(listed >= 0, key_frame * 4 + place, -1).reshape(-1)
    ids = jnp.arange((frames + 2) * 4)
    id_frame, id_pair = ids // 4, ids % 4
    flip = ((id_frame == 0) | (id_frame == frames + 1)) & ((id_pair == 0) | (id_pair == 3)) & ~even
    true_id = jnp.where(flip, id_frame * 4 + 3 - id_pair, ids)
    total = (frames + 2) * 4

    each = lambda b, *_: (b, 0, 0)
    half_block = pl.BlockSpec((1, span, inner), lambda b, *_: (b // 2, 0, 0))
    whole_block = pl.BlockSpec((1, span, inner), each)
    den_block = pl.BlockSpec((1, span, heads), each)
    near = pl.pallas_call(
        functools.partial(near_kernel, slots=slots),
        out_shape=(
            jax.ShapeDtypeStruct((blocks, span, inner), BF),
            jax.ShapeDtypeStruct((blocks, span, inner), F32),
            jax.ShapeDtypeStruct((blocks, span, heads), F32),
            jax.ShapeDtypeStruct((frames + 2, 64, reach), F32),
        ),
        grid_spec=pltpu.PrefetchScalarGridSpec(
            num_scalar_prefetch=2,
            grid=(blocks,),
            in_specs=[VM] * 8 + [half_block] * 2 + [VM] * 4,
            out_specs=(whole_block, whole_block, den_block, VM),
            scratch_shapes=[
                pltpu.VMEM((blocks, span, inner), BF),
                pltpu.VMEM((blocks, span, inner), BF),
                pltpu.VMEM((heads, span, 128), F32),
                pltpu.SMEM((blocks,), jnp.int32),
            ],
        ),
        compiler_params=params(26),
        cost_estimate=pl.CostEstimate(flops=16 * 10**9, bytes_accessed=16 * MIB, transcendentals=0),
    )
    query, num, den, cols = near(
        slot, logit_scale / (inner // heads),
        tall, upper, lower, latent_bias.reshape(-1, 1), gram, rk, rv, rq, qa, qb,
        ka, kb, va, vb,
    )

    def outer(i):
        pick = lambda u, d: jnp.where(even, u[i], d[i])
        return jnp.concatenate([pick(up_k, down_k), pick(up_v, down_v)], axis=-1)[None]

    outer_fwd = shift(outer(-1), "tm", 1)
    outer_back = shift(outer(0), "tm", -1)
    corner = jnp.stack([jnp.where(even, fwd[1], fwd[0]), jnp.where(even, back[1], back[0])])
    corner = swap(corner, "row", 1)

    out = pl.pallas_call(
        functools.partial(far_kernel, slots=slots),
        out_shape=jax.ShapeDtypeStruct((blocks, span, inner), BF),
        grid_spec=pltpu.PrefetchScalarGridSpec(
            num_scalar_prefetch=2,
            grid=(blocks,),
            in_specs=[whole_block, whole_block, den_block, VM, VM, VM] + [ANY] * 9,
            out_specs=whole_block,
            scratch_shapes=[
                pltpu.VMEM((total, span, 2 * inner), BF),
                pltpu.VMEM((total, span, inner), BF),
                pltpu.VMEM((total, span, inner), BF),
                pltpu.VMEM((span, inner), F32),
                pltpu.VMEM((heads, span, 128), F32),
                pltpu.SMEM((total,), jnp.int32),
                pltpu.SemaphoreType.DMA((total,)),
            ],
        ),
        compiler_params=params(38),
    )(
        slot, true_id, query, num, den, cols, rk, rv,
        up_k, down_k, up_v, down_v, fwd, back, outer_fwd, outer_back, corner,
    )
    return out.reshape(frames, slab_rows, row_width, inner)


def solution(mesh):
    in_specs = (
        P("tm", "row", None, None),
        P(),
        P(),
        P(),
        P(),
        P("tm", "row", None),
        P(),
        P(),
        P("tm", "row", None, None),
        P(),
        P(),
        P(),
        P(),
        P("tm", "row", None),
    )
    out_specs = P("tm", "row", None, None)

    return jax.shard_map(
        per_device, mesh=mesh, in_specs=in_specs, out_specs=out_specs, check_vma=False
    )
```
